1024 devices in a mesh: gx: 16 (over z, core), gy: 16 (over y, x_hi), gz: 4 (over x_lo).
Axes of the slice: x: 8 (x_hi: 2, x_lo: 4; x = x_hi * 4 + x_lo), y: 8, z: 8, core: 2. Of those that a mesh axis runs over, the one named last changes fastest.
Arguments:
- spacetime: float32 [22, 64, 64, 512], P(None, 'gx', 'gy', 'gz'), may hold values from -0.2 to 1.12, as said below
- fluid: float32 [8, 64, 64, 512], P(None, 'gx', 'gy', 'gz'), may hold values from -20 to 20, as said below
Outputs:
- spacetime_next: float32 [22, 64, 64, 512], P(None, 'gx', 'gy', 'gz')
- fluid_next: float32 [8, 64, 64, 512], P(None, 'gx', 'gy', 'gz')
The draws below stay inside these ranges and needn't reach their ends.
Inputs may be any that keep to these rules, and one draw needn't show every extreme that they name: `spacetime`: chi and the lapse are positive and at most one; the conformal metric's entries are each within 0.12 of those of the identity. `fluid`: the first five components are densitized conserved values of states with positive density and pressure and speeds below one; the face fields have zero discrete divergence up to rounding.
All inputs are finite; a program needn't handle non-finite values.
Results may differ from the reference program's by a relative error of at most 0.0003.
Values sent between devices are 32-bit elements; how exact they have to be, the bound alone decides.
A program may use at most 32 MiB of HBM per device.

```python
import math
import jax
import jax.numpy as jnp
from jax import lax

FIELDS = 22
GHOST = 3
RECOVERY_STEPS = 4
CX = 4
CY = 4
NX = 64
NY = 64
NZ = 512
N_GX = 16
N_GY = 16


def positions():
    along_x = (jnp.arange(NX, dtype=jnp.float32) / NX)[:, None, None]
    along_y = (jnp.arange(NY, dtype=jnp.float32) / NY)[None, :, None]
    along_z = (jnp.arange(NZ, dtype=jnp.float32) / NZ)[None, None, :]
    return (along_x, along_y, along_z)


def spacetime_fields(key):
    rough_part = jax.random.uniform(jax.random.fold_in(key, 11), (FIELDS, NX, NY, NZ), jnp.float32, -1.0, 1.0)
    along_x, along_y, along_z = positions()
    trend_value = (along_x + along_y + along_z) / 3.0
    identity = [1.0, 0.0, 0.0, 1.0, 0.0, 1.0]
    pieces = [0.75 + 0.25 * rough_part[0]]
    pieces = pieces + [identity[s] + 0.12 * rough_part[1 + s] for s in range(6)]
    pieces = pieces + [(0.3 + 0.6 * trend_value) * (0.85 + 0.15 * rough_part[7])]
    pieces = pieces + [0.1 * rough_part[8 + i] for i in range(3)]
    pieces = pieces + [0.2 * rough_part[11]]
    pieces = pieces + [0.1 * rough_part[12 + s] for s in range(6)]
    pieces = pieces + [0.1 * rough_part[18 + i] for i in range(3)]
    pieces = pieces + [0.05 * rough_part[21]]
    return jnp.stack(pieces)


def draw_spacetime(key, part):
    return spacetime_fields(key)


def draw_fluid(key, part):
    conformal = spacetime_fields(key)[0]
    keys_all = jax.random.split(jax.random.fold_in(key, 23), 4)
    shape_one = (NX, NY, NZ)
    rest_mass = jnp.exp(jax.random.uniform(keys_all[0], shape_one, jnp.float32, math.log(0.2), 0.0))
    pressure = rest_mass * jnp.exp(jax.random.uniform(keys_all[1], shape_one, jnp.float32, math.log(0.0005), math.log(0.4)))
    four_vel = jax.random.uniform(keys_all[2], (3,) + shape_one, jnp.float32, -0.5, 0.5)
    potential = jax.random.uniform(keys_all[3], (3,) + shape_one, jnp.float32, -0.15, 0.15)
    face_fields = []
    for d in range(3):
        e = (d + 1) % 3
        f = (d + 2) % 3
        face_fields.append(jnp.roll(potential[f], -1, axis=e) - potential[f] - jnp.roll(potential[e], -1, axis=f) + potential[e])
    volume = 1.0 / (conformal * jnp.sqrt(conformal))
    magnetic = [0.5 * (face_fields[d] + jnp.roll(face_fields[d], -1, axis=d)) / volume for d in range(3)]
    lorentz = jnp.sqrt(1.0 + four_vel[0] * four_vel[0] + four_vel[1] * four_vel[1] + four_vel[2] * four_vel[2])
    velocity = [four_vel[i] / lorentz for i in range(3)]
    along_b = velocity[0] * magnetic[0] + velocity[1] * magnetic[1] + velocity[2] * magnetic[2]
    time_b = lorentz * along_b
    space_b = [magnetic[i] / lorentz + time_b * velocity[i] for i in range(3)]
    b_square = (magnetic[0] * magnetic[0] + magnetic[1] * magnetic[1] + magnetic[2] * magnetic[2]) / (lorentz * lorentz) + along_b * along_b
    inertia = rest_mass + 2.0 * pressure + b_square
    total_pressure = pressure + 0.5 * b_square
    density = rest_mass * lorentz
    lorentz_sq = lorentz * lorentz
    momenta = [inertia * lorentz_sq * velocity[j] - time_b * space_b[j] for j in range(3)]
    energy = inertia * lorentz_sq - total_pressure - time_b * time_b - density
    return jnp.stack([volume * density] + [volume * member for member in momenta] + [volume * energy] + face_fields)


def setup_inputs(seed: int = 0) -> dict:
    seeds = jax.random.split(jax.random.key(seed), 3)
    spacetime = draw_spacetime(jax.random.fold_in(seeds[2], 71), 0)
    fluid = draw_fluid(jax.random.fold_in(seeds[2], 71), 0)
    return {"spacetime": spacetime, "fluid": fluid}


INDEX_PAIRS = ((0, 0), (0, 1), (0, 2), (1, 1), (1, 2), (2, 2))
FIRST_WEIGHTS = ((-2, 1.0 / 12.0), (-1, -8.0 / 12.0), (1, 8.0 / 12.0), (2, -1.0 / 12.0))
SECOND_WEIGHTS = ((-2, -1.0 / 12.0), (-1, 16.0 / 12.0), (0, -30.0 / 12.0), (1, 16.0 / 12.0), (2, -1.0 / 12.0))
KREISS_WEIGHTS = ((-3, 1.0 / 64.0), (-2, -6.0 / 64.0), (-1, 15.0 / 64.0), (0, -20.0 / 64.0), (1, 15.0 / 64.0), (2, -6.0 / 64.0), (3, 1.0 / 64.0))
COURANT = 0.25
DISSIPATION = 0.2
KAPPA_ONE = 0.02
SHIFT_DAMPING = 1.0
SPEED_CAP = 0.99
PRESSURE_FLOOR = 0.01
FOUR_PI = 4.0 * math.pi

def add_all(pieces):
    summed = pieces[0]
    for member in pieces[1:]:
        summed = summed + member
    return summed

def inner_three(first_vec, second_vec):
    return add_all([first_vec[i] * second_vec[i] for i in range(3)])

def pair_slot(i, j):
    return INDEX_PAIRS.index((min(i, j), max(i, j)))

def symmetric(stack, offset):
    return [[stack[offset + pair_slot(i, j)] for j in range(3)] for i in range(3)]

def full_matrix(table):
    return [[table[min(i, j), max(i, j)] for j in range(3)] for i in range(3)]

def others(direction):
    return [b for b in range(3) if b != direction]

def window(values, direction, low_cut, high_cut):
    position = values.ndim - 3 + direction
    return lax.slice_in_dim(values, low_cut, values.shape[position] - high_cut, axis=position)

def interior(values, directions):
    for direction in directions:
        values = window(values, direction, GHOST, GHOST)
    return values

def stencil(values, direction, weights):
    summed = None
    for offset, weight in weights:
        term_value = weight * window(values, direction, GHOST + offset, GHOST - offset)
        summed = term_value if summed is None else summed + term_value
    return summed

def first_derivs(padded):
    return [stencil(interior(padded, others(a)), a, FIRST_WEIGHTS) for a in range(3)]

def second_derivs(padded):
    result = {}
    for a in range(3):
        for b in range(a, 3):
            if a == b:
                result[a, b] = stencil(interior(padded, others(a)), a, SECOND_WEIGHTS)
            else:
                remaining = [c for c in range(3) if c != a and c != b]
                result[a, b] = stencil(stencil(interior(padded, remaining), a, FIRST_WEIGHTS), b, FIRST_WEIGHTS)
    return result

def dissipation(padded):
    summed = stencil(interior(padded, others(0)), 0, KREISS_WEIGHTS)
    for a in (1, 2):
        summed = summed + stencil(interior(padded, others(a)), a, KREISS_WEIGHTS)
    return DISSIPATION * summed

def inverse_metric(metric):
    cofactor = {}
    cofactor[0, 0] = metric[1][1] * metric[2][2] - metric[1][2] * metric[1][2]
    cofactor[0, 1] = metric[0][2] * metric[1][2] - metric[0][1] * metric[2][2]
    cofactor[0, 2] = metric[0][1] * metric[1][2] - metric[0][2] * metric[1][1]
    cofactor[1, 1] = metric[0][0] * metric[2][2] - metric[0][2] * metric[0][2]
    cofactor[1, 2] = metric[0][1] * metric[0][2] - metric[0][0] * metric[1][2]
    cofactor[2, 2] = metric[0][0] * metric[1][1] - metric[0][1] * metric[0][1]
    determinant = metric[0][0] * cofactor[0, 0] + metric[0][1] * cofactor[0, 1] + metric[0][2] * cofactor[0, 2]
    return full_matrix({pair: cofactor[pair] / determinant for pair in INDEX_PAIRS})

def wave_speed(current):
    inverse = inverse_metric(symmetric(current, 1))
    speeds = [jnp.abs(current[8 + d]) + jnp.sqrt(2.0 * current[7] * current[0] * inverse[d][d]) for d in range(3)]
    return jnp.maximum(jnp.maximum(speeds[0], speeds[1]), speeds[2])

def stress_parts(rest_mass, pressure, four_vel, magnetic):
    lorentz = jnp.sqrt(1.0 + inner_three(four_vel, four_vel))
    velocity = [four_vel[i] / lorentz for i in range(3)]
    along_b = inner_three(velocity, magnetic)
    time_b = lorentz * along_b
    space_b = [magnetic[i] / lorentz + time_b * velocity[i] for i in range(3)]
    b_square = inner_three(magnetic, magnetic) / (lorentz * lorentz) + along_b * along_b
    enthalpy = rest_mass + 2.0 * pressure
    inertia = enthalpy + b_square
    total_pressure = pressure + 0.5 * b_square
    return (lorentz, velocity, time_b, space_b, b_square, enthalpy, inertia, total_pressure)

def face_state(rest_mass, pressure, four_vel, magnetic, d):
    lorentz, velocity, time_b, space_b, b_square, enthalpy, inertia, total_pressure = stress_parts(rest_mass, pressure, four_vel, magnetic)
    lorentz_sq = lorentz * lorentz
    density = rest_mass * lorentz
    conserved = [density] + [inertia * lorentz_sq * velocity[j] - time_b * space_b[j] for j in range(3)]
    conserved = conserved + [inertia * lorentz_sq - total_pressure - time_b * time_b - density]
    flux_list = [density * velocity[d]]
    for j in range(3):
        flux_j = inertia * lorentz_sq * velocity[d] * velocity[j] - space_b[d] * space_b[j]
        if j == d:
            flux_j = flux_j + total_pressure
        flux_list.append(flux_j)
    flux_list.append(inertia * lorentz_sq * velocity[d] - time_b * space_b[d] - density * velocity[d])
    speed_sq = inner_three(velocity, velocity)
    sound_sq = 2.0 * pressure / enthalpy
    alfven_sq = b_square / inertia
    fast_sq = sound_sq + alfven_sq - sound_sq * alfven_sq
    spread = jnp.sqrt(fast_sq * (1.0 - speed_sq) * (1.0 - speed_sq * fast_sq - velocity[d] * velocity[d] * (1.0 - fast_sq)))
    middle = velocity[d] * (1.0 - fast_sq)
    fastest = jnp.maximum(jnp.abs(middle + spread), jnp.abs(middle - spread)) / (1.0 - speed_sq * fast_sq)
    return (conserved, flux_list, fastest)

def recover(conserved, magnetic):
    density = conserved[0]
    momenta = [conserved[1 + i] for i in range(3)]
    energy = conserved[4] + density
    mom_sq = inner_three(momenta, momenta)
    mag_sq = inner_three(magnetic, magnetic)
    cross = inner_three(momenta, magnetic)
    cross_sq = cross * cross

    def recovered_state(guess_z):
        speed_sq = (mom_sq * guess_z * guess_z + cross_sq * (2.0 * guess_z + mag_sq)) / (guess_z * guess_z * (guess_z + mag_sq) * (guess_z + mag_sq))
        inv_lorentz_sq = 1.0 - jnp.minimum(speed_sq, SPEED_CAP)
        rest_mass = density * jnp.sqrt(inv_lorentz_sq)
        pressure = 0.5 * (guess_z * inv_lorentz_sq - rest_mass)
        return (inv_lorentz_sq, rest_mass, pressure)
    guess_z = jnp.maximum(energy - 0.5 * mag_sq, density)
    for attempt in range(RECOVERY_STEPS):
        inv_lorentz_sq, rest_mass, pressure = recovered_state(guess_z)
        residual = guess_z + mag_sq - pressure - 0.5 * mag_sq * inv_lorentz_sq - 0.5 * cross_sq / (guess_z * guess_z) - energy
        guess_z = jnp.maximum(guess_z - residual / (1.0 - 0.5 * inv_lorentz_sq), density)
    inv_lorentz_sq, rest_mass, pressure = recovered_state(guess_z)
    pressure = jnp.maximum(pressure, PRESSURE_FLOOR * rest_mass)
    lorentz = 1.0 / jnp.sqrt(inv_lorentz_sq)
    four_vel = [lorentz * (momenta[i] + cross * magnetic[i] / guess_z) / (guess_z + mag_sq) for i in range(3)]
    return (rest_mass, pressure, four_vel)

def limited(low_side, high_side):
    return 0.5 * (jnp.sign(low_side) + jnp.sign(high_side)) * jnp.minimum(jnp.abs(low_side), jnp.abs(high_side))

def corner_box(values):
    for direction in range(3):
        values = window(values, direction, 0, 1)
    return values

def owned_box(values):
    for direction in range(3):
        values = window(values, direction, GHOST, GHOST - 1)
    return values

def edge_cells(values):
    for direction in range(3):
        values = window(values, direction, GHOST - 1, 1)
    return values

def face_average(values, d):
    paired = window(values, d, GHOST - 1, GHOST - 1)
    return interior(0.5 * (window(paired, d, 0, 1) + window(paired, d, 1, 0)), others(d))

def edge_average(values, d):
    values = window(values, d, 1, 1)
    for e in others(d):
        values = 0.5 * (window(values, e, 0, 1) + window(values, e, 1, 0))
    return values

def edge_difference(edge_vals, d, e):
    edge_vals = window(edge_vals, d, 0, 1)
    return window(edge_vals, e, 1, 0) - window(edge_vals, e, 0, 1)

def fluid_rates(padded_st, padded_fl, current, gradient):
    chi_box = corner_box(padded_st[0])
    volume_box = 1.0 / (chi_box * jnp.sqrt(chi_box))
    centred = []
    for d in range(3):
        averaged = 0.5 * (window(padded_fl[5 + d], d, 0, 1) + window(padded_fl[5 + d], d, 1, 0))
        for e in others(d):
            averaged = window(averaged, e, 0, 1)
        centred.append(averaged)
    magnetic_box = [centred[d] / volume_box for d in range(3)]
    conserved_box = corner_box(padded_fl[:5]) / volume_box
    rest_mass, pressure, four_vel = recover(conserved_box, magnetic_box)
    primitives = jnp.stack([rest_mass, pressure] + four_vel + magnetic_box)
    hydro_rate = [0.0] * 5
    for d in range(3):
        line_prims = window(primitives, d, 1, 0)
        for e in others(d):
            line_prims = window(line_prims, e, GHOST, GHOST - 1)
        low_diff = window(line_prims, d, 1, 1) - window(line_prims, d, 0, 2)
        high_diff = window(line_prims, d, 2, 0) - window(line_prims, d, 1, 1)
        slopes = limited(low_diff, high_diff)
        centre = window(line_prims, d, 1, 1)
        left_state = window(centre, d, 0, 1) + 0.5 * window(slopes, d, 0, 1)
        right_state = window(centre, d, 1, 0) - 0.5 * window(slopes, d, 1, 0)
        lapse_face = face_average(padded_st[7], d)
        chi_face = face_average(padded_st[0], d)
        volume_face = 1.0 / (chi_face * jnp.sqrt(chi_face))
        normal = interior(window(padded_fl[5 + d], d, GHOST, GHOST - 1), others(d)) / volume_face
        fluxes = []
        for one_side in (left_state, right_state):
            magnetic = [one_side[5 + i] for i in range(3)]
            magnetic[d] = normal
            fluxes.append(face_state(one_side[0], one_side[1], [one_side[2], one_side[3], one_side[4]], magnetic, d))
        cons_left, flux_left, fast_left = fluxes[0]
        cons_right, flux_right, fast_right = fluxes[1]
        signal = jnp.maximum(fast_left, fast_right)
        weight = lapse_face * volume_face
        for q in range(5):
            face_flux = weight * (0.5 * (flux_left[q] + flux_right[q]) - 0.5 * signal * (cons_right[q] - cons_left[q]))
            hydro_rate[q] = hydro_rate[q] - (window(face_flux, d, 1, 0) - window(face_flux, d, 0, 1))
    owned_prims = owned_box(primitives)
    lorentz, velocity, time_b, space_b, b_square, enthalpy, inertia, total_pressure = stress_parts(owned_prims[0], owned_prims[1], [owned_prims[2], owned_prims[3], owned_prims[4]], [owned_prims[5], owned_prims[6], owned_prims[7]])
    lorentz_sq = lorentz * lorentz
    stress_pairs = {}
    for i, j in INDEX_PAIRS:
        stress_ij = inertia * lorentz_sq * velocity[i] * velocity[j] - space_b[i] * space_b[j]
        if i == j:
            stress_ij = stress_ij + total_pressure
        stress_pairs[i, j] = stress_ij
    stress = full_matrix(stress_pairs)
    held = interior(padded_fl[:5], (0, 1, 2))
    conformal = current[0]
    volume = 1.0 / (conformal * jnp.sqrt(conformal))
    lapse_now = current[7]
    lapse_grad = [gradient[k][7] for k in range(3)]
    trace_total = current[11] + 2.0 * current[21]
    metric = symmetric(current, 1)
    traceless = symmetric(current, 12)
    curv_phys = full_matrix({pair: (traceless[pair[0]][pair[1]] + metric[pair[0]][pair[1]] * trace_total / 3.0) / conformal for pair in INDEX_PAIRS})
    total_energy = held[4] + held[0]
    for i in range(3):
        hydro_rate[1 + i] = hydro_rate[1 + i] - total_energy * lapse_grad[i] + add_all([held[1 + k] * gradient[i][8 + k] for k in range(3)])
    hydro_rate[4] = hydro_rate[4] + lapse_now * volume * add_all([stress[i][j] * curv_phys[i][j] for i in range(3) for j in range(3)]) - add_all([held[1 + j] * lapse_grad[j] for j in range(3)])
    matter = {'energy': total_energy / volume, 'momentum': [held[1 + i] / volume for i in range(3)], 'stress': stress}
    four_edge = [edge_cells(four_vel[i]) for i in range(3)]
    lorentz_edge = jnp.sqrt(1.0 + inner_three(four_edge, four_edge))
    vel_edge = [four_edge[i] / lorentz_edge for i in range(3)]
    mag_edge = [edge_cells(centred[i]) for i in range(3)]
    lapse_cells = padded_st[7]
    for direction in range(3):
        lapse_cells = window(lapse_cells, direction, GHOST - 1, GHOST - 1)
    electric = [-lapse_cells * (vel_edge[(i + 1) % 3] * mag_edge[(i + 2) % 3] - vel_edge[(i + 2) % 3] * mag_edge[(i + 1) % 3]) for i in range(3)]
    edge_vals = [edge_average(electric[i], i) for i in range(3)]
    field_rate = []
    for d in range(3):
        e = (d + 1) % 3
        f = (d + 2) % 3
        field_rate.append(-(edge_difference(edge_vals[f], d, e) - edge_difference(edge_vals[e], d, f)))
    return (hydro_rate, field_rate, matter)

def z4c_rates(padded_st, current, gradient, matter):
    curvature = second_derivs(padded_st[:11])

    def hessian(field, a, b):
        return curvature[min(a, b), max(a, b)][field]
    conformal = current[0]
    metric = symmetric(current, 1)
    lapse_now = current[7]
    shift_vec = [current[8 + i] for i in range(3)]
    extrinsic = current[11]
    traceless = symmetric(current, 12)
    connection = [current[18 + i] for i in range(3)]
    z_theta = current[21]
    inverse = inverse_metric(metric)
    metric_grad = [[[gradient[k][1 + pair_slot(i, j)] for j in range(3)] for i in range(3)] for k in range(3)]
    lowered = [[[0.5 * (metric_grad[j][i][k] + metric_grad[k][i][j] - metric_grad[i][j][k]) for k in range(3)] for j in range(3)] for i in range(3)]
    raised = [[[add_all([inverse[i][l] * lowered[l][j][k] for l in range(3)]) for k in range(3)] for j in range(3)] for i in range(3)]
    contracted = [add_all([inverse[j][k] * raised[i][j][k] for j in range(3) for k in range(3)]) for i in range(3)]
    chi_grad = [gradient[k][0] for k in range(3)]
    lapse_grad = [gradient[k][7] for k in range(3)]
    chi_cov = full_matrix({pair: hessian(0, pair[0], pair[1]) - add_all([raised[k][pair[0]][pair[1]] * chi_grad[k] for k in range(3)]) for pair in INDEX_PAIRS})
    chi_lap = add_all([inverse[i][j] * chi_cov[i][j] for i in range(3) for j in range(3)])
    chi_square = add_all([inverse[i][j] * chi_grad[i] * chi_grad[j] for i in range(3) for j in range(3)])
    cross_term = add_all([inverse[i][j] * chi_grad[i] * lapse_grad[j] for i in range(3) for j in range(3)])
    lapse_cov = full_matrix({pair: hessian(7, pair[0], pair[1]) - add_all([raised[k][pair[0]][pair[1]] * lapse_grad[k] for k in range(3)]) + (chi_grad[pair[0]] * lapse_grad[pair[1]] + chi_grad[pair[1]] * lapse_grad[pair[0]] - metric[pair[0]][pair[1]] * cross_term) / (2.0 * conformal) for pair in INDEX_PAIRS})
    lapse_lap = conformal * add_all([inverse[i][j] * lapse_cov[i][j] for i in range(3) for j in range(3)])
    ricci_pairs = {}
    for i, j in INDEX_PAIRS:
        slot_index = 1 + pair_slot(i, j)
        second_part = -0.5 * add_all([inverse[l][m] * hessian(slot_index, l, m) for l in range(3) for m in range(3)])
        connection_part = 0.5 * add_all([metric[k][i] * gradient[j][18 + k] + metric[k][j] * gradient[i][18 + k] for k in range(3)])
        contracted_part = 0.5 * add_all([contracted[k] * (lowered[i][j][k] + lowered[j][i][k]) for k in range(3)])
        quadratic = add_all([inverse[l][m] * (raised[k][l][i] * lowered[j][k][m] + raised[k][l][j] * lowered[i][k][m] + raised[k][i][m] * lowered[k][l][j]) for l in range(3) for m in range(3) for k in range(3)])
        conformal_part = (chi_cov[i][j] + metric[i][j] * chi_lap) / (2.0 * conformal) - (chi_grad[i] * chi_grad[j] + 3.0 * metric[i][j] * chi_square) / (4.0 * conformal * conformal)
        ricci_pairs[i, j] = second_part + connection_part + contracted_part + quadratic + conformal_part
    ricci_ten = full_matrix(ricci_pairs)
    ricci_scalar = conformal * add_all([inverse[i][j] * ricci_ten[i][j] for i in range(3) for j in range(3)])
    stress = matter['stress']
    density_adm = matter['energy']
    momentum = matter['momentum']
    stress_trace = conformal * add_all([inverse[i][j] * stress[i][j] for i in range(3) for j in range(3)])
    raised_a = full_matrix({pair: add_all([inverse[pair[0]][k] * inverse[pair[1]][l] * traceless[k][l] for k in range(3) for l in range(3)]) for pair in INDEX_PAIRS})
    a_square = add_all([traceless[i][j] * raised_a[i][j] for i in range(3) for j in range(3)])
    shift_grad = [[gradient[k][8 + i] for i in range(3)] for k in range(3)]
    shift_div = add_all([shift_grad[k][k] for k in range(3)])
    trace_total = extrinsic + 2.0 * z_theta

    def advect(field):
        return add_all([shift_vec[k] * gradient[k][field] for k in range(3)])
    rate_list = [None] * current.shape[0]
    rate_list[0] = advect(0) + 2.0 / 3.0 * conformal * (lapse_now * trace_total - shift_div)
    rate_list[7] = advect(7) - 2.0 * lapse_now * extrinsic
    for i in range(3):
        rate_list[8 + i] = advect(8 + i) + 0.75 * connection[i] - SHIFT_DAMPING * shift_vec[i]
    rate_list[11] = advect(11) - lapse_lap + lapse_now * (a_square + trace_total * trace_total / 3.0) + FOUR_PI * lapse_now * (stress_trace + density_adm) + KAPPA_ONE * lapse_now * z_theta
    source = [[-lapse_cov[i][j] + lapse_now * (ricci_ten[i][j] - 2.0 * FOUR_PI * stress[i][j]) for j in range(3)] for i in range(3)]
    source_trace = add_all([inverse[i][j] * source[i][j] for i in range(3) for j in range(3)])
    for i, j in INDEX_PAIRS:
        slot_index = pair_slot(i, j)
        rate_list[1 + slot_index] = advect(1 + slot_index) + add_all([metric[i][k] * shift_grad[j][k] + metric[j][k] * shift_grad[i][k] for k in range(3)]) - 2.0 / 3.0 * metric[i][j] * shift_div - 2.0 * lapse_now * traceless[i][j]
        product = add_all([traceless[i][k] * inverse[k][l] * traceless[l][j] for k in range(3) for l in range(3)])
        rate_list[12 + slot_index] = advect(12 + slot_index) + add_all([traceless[i][k] * shift_grad[j][k] + traceless[j][k] * shift_grad[i][k] for k in range(3)]) - 2.0 / 3.0 * traceless[i][j] * shift_div + conformal * (source[i][j] - metric[i][j] * source_trace / 3.0) + lapse_now * (trace_total * traceless[i][j] - 2.0 * product)
    for i in range(3):
        bracket = add_all([raised[i][j][k] * raised_a[j][k] for j in range(3) for k in range(3)])
        bracket = bracket - 1.5 * add_all([raised_a[i][j] * chi_grad[j] for j in range(3)]) / conformal
        bracket = bracket - add_all([inverse[i][j] * (2.0 * gradient[j][11] + gradient[j][21]) for j in range(3)]) / 3.0
        bracket = bracket - 2.0 * FOUR_PI * add_all([inverse[i][j] * momentum[j] for j in range(3)])
        rate_list[18 + i] = advect(18 + i) - add_all([contracted[j] * shift_grad[j][i] for j in range(3)]) + 2.0 / 3.0 * contracted[i] * shift_div + add_all([inverse[j][k] * hessian(8 + i, j, k) for j in range(3) for k in range(3)]) + add_all([inverse[i][j] * hessian(8 + k, j, k) for j in range(3) for k in range(3)]) / 3.0 - 2.0 * add_all([raised_a[i][j] * lapse_grad[j] for j in range(3)]) + 2.0 * lapse_now * bracket - 2.0 * KAPPA_ONE * lapse_now * (connection[i] - contracted[i])
    rate_list[21] = advect(21) + 0.5 * lapse_now * (ricci_scalar - a_square + 2.0 / 3.0 * trace_total * trace_total - 4.0 * FOUR_PI * density_adm) - 2.0 * KAPPA_ONE * lapse_now * z_theta
    return jnp.stack(rate_list) + dissipation(padded_st)

def tendencies(padded_st, padded_fl):
    gradient = first_derivs(padded_st)
    current = interior(padded_st, (0, 1, 2))
    hydro_rate, field_rate, matter = fluid_rates(padded_st, padded_fl, current, gradient)
    spacetime_rate = z4c_rates(padded_st, current, gradient, matter)
    return (spacetime_rate, jnp.stack(hydro_rate + field_rate))

def regroup(rates, count):
    rates = rates.reshape((N_GX, N_GY, count, CX, CY, rates.shape[-1]))
    rates = jnp.transpose(rates, (2, 0, 3, 1, 4, 5))
    return rates.reshape((count, N_GX * CX, N_GY * CY, rates.shape[-1]))

def reference(spacetime, fluid):
    timestep = COURANT / jnp.max(wave_speed(spacetime))
    widths = ((0, 0), (GHOST, GHOST), (GHOST, GHOST), (GHOST, GHOST))
    padded_st = jnp.pad(spacetime, widths, mode='wrap')
    padded_fl = jnp.pad(fluid, widths, mode='wrap')

    def block_rates(block_index):
        offset_x = block_index // N_GY * CX
        offset_y = block_index % N_GY * CY
        block_st = lax.dynamic_slice_in_dim(padded_st, offset_x, CX + 2 * GHOST, axis=1)
        block_st = lax.dynamic_slice_in_dim(block_st, offset_y, CY + 2 * GHOST, axis=2)
        block_fl = lax.dynamic_slice_in_dim(padded_fl, offset_x, CX + 2 * GHOST, axis=1)
        block_fl = lax.dynamic_slice_in_dim(block_fl, offset_y, CY + 2 * GHOST, axis=2)
        return tendencies(block_st, block_fl)
    spacetime_rate, fluid_rate = lax.map(block_rates, jnp.arange(N_GX * N_GY, dtype=jnp.int32))
    spacetime_rate = regroup(spacetime_rate, spacetime.shape[0])
    fluid_rate = regroup(fluid_rate, fluid.shape[0])
    return (spacetime + timestep * spacetime_rate, fluid + timestep * fluid_rate)
```

```python
import math
import jax
import jax.numpy as jnp
from jax import lax
from jax.experimental import pallas as pl
from jax.experimental.pallas import tpu as pltpu
from jax.sharding import PartitionSpec as P

RECOVERY_STEPS = 4
PAIRS = ((0, 0), (0, 1), (0, 2), (1, 1), (1, 2), (2, 2))
FOUR_PI = 4.0 * math.pi
PACK = 87
PADX, PADY = 10, 12
NSEC = 4


def slot(i, j):
    return PAIRS.index((min(i, j), max(i, j)))


def row_of(t, xp, yp):
    return ((t * PADX + xp) * PADY + yp) * 8


def lanes():
    return lax.broadcasted_iota(jnp.int32, (8, 128), 1)


def rows_iota():
    return lax.broadcasted_iota(jnp.int32, (8, 128), 0)


def lroll(v, amount):
    amount = amount % 128
    return v if amount == 0 else pltpu.roll(v, amount, 1)


def shifted(f, halo, k, lane):
    if k > 0:
        return lroll(jnp.where(lane < k, halo, f), 128 - k)
    return lroll(jnp.where(lane >= 128 + k, halo, f), -k)


def d_one(m2, m1, p1, p2):
    return (8.0 / 12.0) * (p1 - m1) - (1.0 / 12.0) * (p2 - m2)


def line_derivs(v, second):
    s1 = v[1] + v[-1]
    s2 = v[2] + v[-2]
    s3 = v[3] + v[-3]
    first = (8.0 / 12.0) * (v[1] - v[-1]) - (1.0 / 12.0) * (v[2] - v[-2])
    kreiss = (0.2 / 64.0) * s3 - (0.2 * 6.0 / 64.0) * s2 + (0.2 * 15.0 / 64.0) * s1
    sec = None
    if second:
        sec = (16.0 / 12.0) * s1 - (1.0 / 12.0) * s2 - (30.0 / 12.0) * v[0]
    return first, kreiss, sec


def fanned(v, amount):
    if amount + 21 >= 128:
        v, amount = lroll(v, amount), 0
    return pltpu.roll(v, amount, 1, stride=3, stride_axis=0)


def expand(lo, hi, t, lane):
    up = fanned(hi, 128 - PACK + 24 * t)
    dn = fanned(lo, 125 - PACK + 24 * t)
    return jnp.where(lane < 3, up, dn)


def deriv_stage(T, G):
    lane = lanes()

    def tile(t, xp, yp):
        return T[pl.ds(pl.multiple_of(row_of(t, xp, yp), 8), 8), :]

    def packed(xp, yp):
        base = row_of(3, xp, yp)
        lo = jnp.broadcast_to(T[pl.ds(base + 6, 1), :], (8, 128))
        hi = jnp.broadcast_to(T[pl.ds(base + 7, 1), :], (8, 128))
        return lo, hi

    def body(xy, carry):
        x = xy // 4
        y = xy % 4
        xp, yp = x + 3, y + 4
        own_z = packed(xp, yp)
        zx = [packed(xp + a, yp) for a in (-2, -1, 1, 2)]
        zy = [packed(xp, yp + a) for a in (-2, -1, 1, 2)]
        dx_z = [d_one(*[zx[i][side] for i in range(4)]) for side in range(2)]
        dy_z = [d_one(*[zy[i][side] for i in range(4)]) for side in range(2)]

        def put(q, t, value):
            G[pl.ds(pl.multiple_of(((q * 3 + t - 1) * 16 + xy) * 8, 8), 8), :] = value

        for t in (1, 2, 3):
            second = t < 3
            vx = {a: tile(t, xp + a, yp) for a in range(-3, 4)}
            vy = {a: tile(t, xp, yp + a) if a else vx[0] for a in range(-3, 4)}
            halo = expand(own_z[0], own_z[1], t, lane)
            vz = {a: shifted(vx[0], halo, a, lane) if a else vx[0] for a in range(-3, 4)}
            dx, kx, sx = line_derivs(vx, second)
            dy, ky, sy = line_derivs(vy, second)
            dz, kz, sz = line_derivs(vz, second)
            put(0, t, dx)
            put(1, t, dy)
            put(2, t, dz)
            put(3, t, kx + ky + kz - (0.2 * 60.0 / 64.0) * vx[0])
            if second:
                rows = [
                    d_one(*[tile(t, xp + a, yp + b) for b in (-2, -1, 1, 2)])
                    for a in (-2, -1, 1, 2)
                ]
                put(4, t, sx)
                put(5, t, d_one(*rows))
                hx = expand(dx_z[0], dx_z[1], t, lane)
                hy = expand(dy_z[0], dy_z[1], t, lane)
                put(6, t, d_one(*[shifted(dx, hx, a, lane) for a in (-2, -1, 1, 2)]))
                put(7, t, sy)
                put(8, t, d_one(*[shifted(dy, hy, a, lane) for a in (-2, -1, 1, 2)]))
                put(9, t, sz)
        return carry

    lax.fori_loop(0, 16, body, 0)


def dot3(a, b):
    return a[0] * b[0] + a[1] * b[1] + a[2] * b[2]


def recover(cons, mag):
    density = cons[0]
    mom = cons[1:4]
    energy = cons[4] + density
    mom_sq = dot3(mom, mom)
    mag_sq = dot3(mag, mag)
    cross = dot3(mom, mag)
    cross_sq = cross * cross

    def state(z):
        zb = z + mag_sq
        zz = z * z
        speed_sq = (mom_sq * zz + cross_sq * (2.0 * z + mag_sq)) / (zz * zb * zb)
        ilsq = 1.0 - jnp.minimum(speed_sq, 0.99)
        rho = density * jnp.sqrt(ilsq)
        return ilsq, rho, 0.5 * (z * ilsq - rho)

    z = jnp.maximum(energy - 0.5 * mag_sq, density)
    for _ in range(RECOVERY_STEPS):
        ilsq, rho, p = state(z)
        res = z + mag_sq - p - 0.5 * mag_sq * ilsq - 0.5 * cross_sq / (z * z) - energy
        z = jnp.maximum(z - res / (1.0 - 0.5 * ilsq), density)
    ilsq, rho, p = state(z)
    p = jnp.maximum(p, 0.01 * rho)
    lor = 1.0 / jnp.sqrt(ilsq)
    factor = lor / (z + mag_sq)
    cz = cross / z
    return rho, p, [factor * (mom[i] + cz * mag[i]) for i in range(3)]


def prim_stage(T, PR, PH, EC, EH):
    lane = lanes()

    def strip(t, s, xp, dy=0):
        return T[pl.ds(row_of(t, xp + 1, 2 + dy) + s, 8, stride=8), :]

    def finish(cons, low, up, chi, lapse):
        root = chi * jnp.sqrt(chi)
        centred = [0.5 * (low[i] + up[i]) for i in range(3)]
        mag = [c * root for c in centred]
        rho, p, u = recover([c * root for c in cons], mag)
        inv = -lapse / jnp.sqrt(1.0 + dot3(u, u))
        vel = [a * inv for a in u]
        ele = [
            vel[(i + 1) % 3] * centred[(i + 2) % 3] - vel[(i + 2) % 3] * centred[(i + 1) % 3]
            for i in range(3)
        ]
        return [rho, p] + u + mag, ele

    def body(xp, carry):
        own = [strip(0, s, xp) for s in range(8)]
        zhi = strip(3, 7, xp)
        upper = [
            strip(0, 5, xp + 1),
            strip(0, 6, xp, 1),
            jnp.where(lane == 127, lroll(zhi, 127 - (PACK - 21)), lroll(own[7], 127)),
        ]
        prims, ele = finish(own[:5], own[5:], upper, strip(1, 0, xp), strip(1, 7, xp))
        at = pl.ds(pl.multiple_of(8 + xp * 8, 8), 8)
        for q in range(8):
            PR[q, at, :] = prims[q]
        for i in range(3):
            EC[i, at, :] = ele[i]
        return carry

    lax.fori_loop(0, 8, body, 0)

    def body_h(k, carry):
        xp = k + 1

        def halo(u, xq, dy=0):
            p = PACK - 3 * u
            return jnp.where(
                lane < 3, lroll(strip(3, 7, xq, dy), -p), lroll(strip(3, 6, xq, dy), 125 - p)
            )

        vals = [halo(u, xp) for u in range(9)]
        first = T[pl.ds(row_of(0, xp + 1, 2) + 7, 8, stride=8), :]
        upper = [
            halo(5, xp + 1),
            halo(6, xp, 1),
            lroll(jnp.where(lane == 0, first, vals[7]), 127),
        ]
        prims, ele = finish(vals[:5], vals[5:8], upper, vals[8], halo(15, xp))
        at = pl.ds(pl.multiple_of(8 + k * 8, 8), 8)
        for q in range(8):
            PH[q, at, :] = prims[q]
        for i in range(3):
            EH[i, at, :] = ele[i]
        return carry

    lax.fori_loop(0, 6, body_h, 0)


def limited(a, b):
    return jnp.maximum(jnp.minimum(a, b), 0.0) + jnp.minimum(jnp.maximum(a, b), 0.0)


def stress_parts(rho, p, u, mag):
    lor_sq = 1.0 + dot3(u, u)
    lor = jnp.sqrt(lor_sq)
    inv = 1.0 / lor
    vel = [a * inv for a in u]
    along = dot3(vel, mag)
    b0 = lor * along
    b = [mag[i] * inv + b0 * vel[i] for i in range(3)]
    bsq = dot3(mag, mag) * (inv * inv) + along * along
    enth = rho + 2.0 * p
    inertia = enth + bsq
    return lor, lor_sq, vel, b0, b, bsq, enth, inertia, p + 0.5 * bsq


def face_state(rho, p, u, mag, d):
    lor, lor_sq, vel, b0, b, bsq, enth, inertia, ptot = stress_parts(rho, p, u, mag)
    dens = rho * lor
    wl = inertia * lor_sq
    mom = [wl * vel[j] - b0 * b[j] for j in range(3)]
    cons = [dens] + mom + [wl - ptot - b0 * b0 - dens]
    wv = wl * vel[d]
    flux = [dens * vel[d]]
    for j in range(3):
        f = wv * vel[j] - b[d] * b[j]
        flux.append(f + ptot if j == d else f)
    flux.append(mom[d] - dens * vel[d])
    vsq = dot3(vel, vel)
    cs = 2.0 * p / enth
    va = bsq / inertia
    a2 = cs + va - cs * va
    vd = vel[d]
    spread = jnp.sqrt(a2 * (1.0 - vsq) * (1.0 - vsq * a2 - vd * vd * (1.0 - a2)))
    mid = vd * (1.0 - a2)
    fast = jnp.maximum(jnp.abs(mid + spread), jnp.abs(mid - spread)) / (1.0 - vsq * a2)
    return cons, flux, fast


def face_flux(left, right, normal, chi, lapse, d):
    root = chi * jnp.sqrt(chi)
    states = []
    for side in (left, right):
        mag = list(side[5:8])
        mag[d] = normal * root
        states.append(face_state(side[0], side[1], side[2:5], mag, d))
    (cl, fl, sl), (cr, fr, sr) = states
    sig = jnp.maximum(sl, sr)
    weight = 0.5 * lapse / root
    return [weight * (fl[q] + fr[q] - sig * (cr[q] - cl[q])) for q in range(5)]


def recon(m2, m1, c0, p1):
    mid = c0 - m1
    return m1 + 0.5 * limited(m1 - m2, mid), c0 - 0.5 * limited(mid, p1 - c0)


def flux_stage(T, PR, PH, FX, HR):
    lane = lanes()

    def strip(t, s, x, dy=0):
        return T[pl.ds(row_of(t, x + 3, 2 + dy) + s, 8, stride=8), :]

    def prim(q, x, dy=0):
        return PR[q, pl.ds(8 + (x + 2) * 8 + dy, 8), :]

    def half(a, b):
        return 0.5 * (a + b)

    def body_x(i, carry):
        both = [recon(*[prim(q, i + a) for a in (-2, -1, 0, 1)]) for q in range(8)]
        chi = half(strip(1, 0, i - 1), strip(1, 0, i))
        lapse = half(strip(1, 7, i - 1), strip(1, 7, i))
        out = face_flux([b[0] for b in both], [b[1] for b in both], strip(0, 5, i), chi, lapse, 0)
        at = pl.ds(pl.multiple_of(i * 8, 8), 8)
        for q in range(5):
            FX[q, at, :] = out[q]
        return carry

    lax.fori_loop(0, 5, body_x, 0)

    def body(x, carry):
        at = pl.ds(pl.multiple_of(x * 8, 8), 8)
        up = pl.ds(pl.multiple_of(x * 8 + 8, 8), 8)
        chi0, lapse0 = strip(1, 0, x), strip(1, 7, x)
        both = [recon(*[prim(q, x, a) for a in (-2, -1, 0, 1)]) for q in range(8)]
        chi = half(strip(1, 0, x, -1), chi0)
        lapse = half(strip(1, 7, x, -1), lapse0)
        fy = face_flux([b[0] for b in both], [b[1] for b in both], strip(0, 6, x), chi, lapse, 1)
        zlo, zhi = strip(3, 6, x), strip(3, 7, x)

        def halo(u):
            p = PACK - 3 * u
            return jnp.where(lane < 3, lroll(zhi, -p), lroll(zlo, 125 - p))

        chih, lapseh = halo(8), halo(15)
        own = [prim(q, x) for q in range(8)]
        hal = [PH[q, pl.ds(pl.multiple_of(8 + (x + 1) * 8, 8), 8), :] for q in range(8)]
        both = [
            recon(
                shifted(own[q], hal[q], -2, lane),
                shifted(own[q], hal[q], -1, lane),
                own[q],
                shifted(own[q], hal[q], 1, lane),
            )
            for q in range(8)
        ]
        bz = strip(0, 7, x)
        fz = face_flux(
            [b[0] for b in both],
            [b[1] for b in both],
            bz,
            half(shifted(chi0, chih, -1, lane), chi0),
            half(shifted(lapse0, lapseh, -1, lane), lapse0),
            2,
        )
        both = [
            recon(lroll(own[q], 2), lroll(own[q], 1), hal[q], lroll(hal[q], 127)) for q in range(8)
        ]
        fl = face_flux(
            [b[0] for b in both],
            [b[1] for b in both],
            halo(7),
            half(lroll(chi0, 1), chih),
            half(lroll(lapse0, 1), lapseh),
            2,
        )
        for q in range(5):
            FX[5 + q, at, :] = fy[q]
        for q in range(5):
            fzu = lroll(jnp.where(lane == 0, fl[q], fz[q]), 127)
            fyu = FX[5 + q, pl.ds(x * 8 + 1, 8), :]
            HR[q, at, :] = (fz[q] - fzu) + (fy[q] - fyu) + (FX[q, at, :] - FX[q, up, :])
        return carry

    lax.fori_loop(0, 4, body, 0)


def field_stage(EC, EH, EZ, HR):
    lane = lanes()

    def ec(i, x, dy=0):
        return EC[i, pl.ds(8 + (x + 2) * 8 + dy, 8), :]

    def eh(i, x, dy=0):
        return EH[i, pl.ds(8 + (x + 1) * 8 + dy, 8), :]

    for x in range(5):
        at = pl.ds(x * 8, 8)
        EZ[0, at, :] = 0.25 * (ec(2, x - 1, -1) + ec(2, x, -1) + ec(2, x - 1) + ec(2, x))
        s = ec(1, x - 1) + ec(1, x)
        h = eh(1, x - 1) + eh(1, x)
        EZ[1, at, :] = 0.25 * (shifted(s, h, -1, lane) + s)
        EZ[2, at, :] = 0.25 * (shifted(s, h, 1, lane) + s)
        if x < 4:
            s = ec(0, x, -1) + ec(0, x)
            h = eh(0, x, -1) + eh(0, x)
            EZ[3, at, :] = 0.25 * (shifted(s, h, -1, lane) + s)
            EZ[4, at, :] = 0.25 * (shifted(s, h, 1, lane) + s)
    for x in range(4):
        at, up, yu = pl.ds(x * 8, 8), pl.ds(x * 8 + 8, 8), pl.ds(x * 8 + 1, 8)
        ez = EZ[0, at, :]
        HR[5, at, :] = (EZ[2, at, :] - EZ[1, at, :]) - (EZ[0, yu, :] - ez)
        HR[6, at, :] = (EZ[0, up, :] - ez) - (EZ[4, at, :] - EZ[3, at, :])
        HR[7, at, :] = (EZ[3, yu, :] - EZ[3, at, :]) - (EZ[1, up, :] - EZ[1, at, :])


def sym(values):
    return [[values[slot(i, j)] for j in range(3)] for i in range(3)]


def trace(inv, m):
    return (
        inv[0][0] * m[0][0]
        + inv[1][1] * m[1][1]
        + inv[2][2] * m[2][2]
        + 2.0 * (inv[0][1] * m[0][1] + inv[0][2] * m[0][2] + inv[1][2] * m[1][2])
    )


def inverse(g):
    c00 = g[1][1] * g[2][2] - g[1][2] * g[1][2]
    c01 = g[0][2] * g[1][2] - g[0][1] * g[2][2]
    c02 = g[0][1] * g[1][2] - g[0][2] * g[1][1]
    c11 = g[0][0] * g[2][2] - g[0][2] * g[0][2]
    c12 = g[0][1] * g[0][2] - g[0][0] * g[1][2]
    c22 = g[0][0] * g[1][1] - g[0][1] * g[0][1]
    r = 1.0 / (g[0][0] * c00 + g[0][1] * c01 + g[0][2] * c02)
    return sym([c00 * r, c01 * r, c02 * r, c11 * r, c12 * r, c22 * r])


R3 = range(3)


def algebra_stage(G, PR, HR, o_st, o_fl, RT):
    low = rows_iota() < 4

    def body(h, carry):
        x = 2 * h

        def fold(a, b):
            return jnp.where(low, a, b)

        at = pl.ds(pl.multiple_of(8 * h, 8), 8)

        def strip(ref, q, pad):
            return fold(
                ref[q, pl.ds(pad + x * 8 + 2, 8), :], ref[q, pl.ds(pad + x * 8 + 8 - 2, 8), :]
            )

        def g(q, v):
            return G[pl.ds(((q * 3 + v // 8) * 16 + 8 * h) * 8 + v % 8, 8, stride=8), :]

        cur = [o_st[v, at, :] for v in range(22)]
        flu = [o_fl[v, at, :] for v in range(8)]
        prims = [strip(PR, q, 8 + 16) for q in range(8)]

        def grad(v):
            return [g(k, v) for k in R3]

        def hess(v):
            return sym([g(4 + s, v) for s in range(6)])

        chi, lapse = cur[0], cur[7]
        metric = sym(cur[1:7])
        shift = cur[8:11]
        khat, theta = cur[11], cur[21]
        trl = sym(cur[12:18])
        conn = cur[18:21]
        inv = inverse(metric)
        ichi = 1.0 / chi
        root = chi * jnp.sqrt(chi)
        ktot = khat + 2.0 * theta

        lor, lor_sq, vel, b0, b, bsq, enth, inertia, ptot = stress_parts(
            prims[0], prims[1], prims[2:5], prims[5:8]
        )
        wl = inertia * lor_sq
        stress = sym(
            [
                wl * vel[i] * vel[j] - b[i] * b[j] + (ptot if i == j else 0.0)
                for i, j in PAIRS
            ]
        )
        total = flu[4] + flu[0]
        dens = total * root
        mom = [flu[1 + i] * root for i in R3]
        dal = grad(7)
        dsh = [grad(8 + i) for i in R3]
        hydro = [strip(HR, q, 0) for q in range(8)]
        for i in R3:
            hydro[1 + i] = (
                hydro[1 + i]
                - total * dal[i]
                + (flu[1] * dsh[0][i] + flu[2] * dsh[1][i] + flu[3] * dsh[2][i])
            )
        third = ktot * (1.0 / 3.0)
        curv = sym([(trl[i][j] + metric[i][j] * third) * ichi for i, j in PAIRS])
        tk = (
            stress[0][0] * curv[0][0]
            + stress[1][1] * curv[1][1]
            + stress[2][2] * curv[2][2]
            + 2.0
            * (stress[0][1] * curv[0][1] + stress[0][2] * curv[0][2] + stress[1][2] * curv[1][2])
        )
        hydro[4] = hydro[4] + lapse / root * tk - dot3(flu[1:4], dal)
        for q in range(8):
            RT[22 + q, at, :] = hydro[q]

        def adv(gr):
            return shift[0] * gr[0] + shift[1] * gr[1] + shift[2] * gr[2]

        def emit(v, rate):
            RT[v, at, :] = rate + g(3, v)

        dg = [[grad(1 + slot(i, j)) if i <= j else None for j in R3] for i in R3]
        dg = [[dg[min(i, j)][max(i, j)] for j in R3] for i in R3]
        lowered = [
            sym([0.5 * (dg[i][k][j] + dg[i][j][k] - dg[j][k][i]) for j, k in PAIRS]) for i in R3
        ]
        raised = [
            sym(
                [
                    inv[i][0] * lowered[0][j][k]
                    + inv[i][1] * lowered[1][j][k]
                    + inv[i][2] * lowered[2][j][k]
                    for j, k in PAIRS
                ]
            )
            for i in R3
        ]
        gd = [trace(inv, raised[i]) for i in R3]
        dchi = grad(0)
        hchi = hess(0)
        xcov = sym(
            [hchi[i][j] - dot3([raised[k][i][j] for k in R3], dchi) for i, j in PAIRS]
        )
        chi_lap = trace(inv, xcov)
        uchi = [dot3(inv[i], dchi) for i in R3]
        chi_sq = dot3(uchi, dchi)
        cross = dot3(uchi, dal)
        hal = hess(7)
        half_ichi = 0.5 * ichi
        lcov = sym(
            [
                hal[i][j]
                - dot3([raised[k][i][j] for k in R3], dal)
                + (dchi[i] * dal[j] + dchi[j] * dal[i] - metric[i][j] * cross) * half_ichi
                for i, j in PAIRS
            ]
        )
        lapse_lap = chi * trace(inv, lcov)
        dgam = [grad(18 + i) for i in R3]
        cu = [
            [
                [
                    inv[l][0] * lowered[j][k][0]
                    + inv[l][1] * lowered[j][k][1]
                    + inv[l][2] * lowered[j][k][2]
                    for l in R3
                ]
                for k in R3
            ]
            for j in R3
        ]
        quarter = half_ichi * half_ichi
        ricci = []
        for i, j in PAIRS:
            v = 1 + slot(i, j)
            hg = hess(v)
            r = -0.5 * trace(inv, hg)
            for k in R3:
                r = r + 0.5 * (metric[k][i] * dgam[k][j] + metric[k][j] * dgam[k][i])
                r = r + 0.5 * gd[k] * (lowered[i][j][k] + lowered[j][i][k])
            for k in R3:
                for l in R3:
                    r = r + raised[k][l][i] * cu[j][k][l]
                    r = r + raised[k][l][j] * cu[i][k][l]
                    r = r + raised[k][i][l] * cu[k][j][l]
            r = r + (xcov[i][j] + metric[i][j] * chi_lap) * half_ichi
            r = r - (dchi[i] * dchi[j] + 3.0 * metric[i][j] * chi_sq) * quarter
            ricci.append(r)
        ricci = sym(ricci)
        rscal = chi * trace(inv, ricci)
        strace = chi * trace(inv, stress)
        mixed = [[dot3(inv[i], [trl[k][j] for k in R3]) for j in R3] for i in R3]
        up = sym([dot3(mixed[i], inv[j]) for i, j in PAIRS])
        aa = trace(trl, up)
        div = dsh[0][0] + dsh[1][1] + dsh[2][2]
        div23 = (2.0 / 3.0) * div

        emit(0, adv(dchi) + (2.0 / 3.0) * chi * (lapse * ktot - div))
        emit(7, adv(dal) - 2.0 * lapse * khat)
        for i in R3:
            emit(8 + i, adv(dsh[i]) + 0.75 * conn[i] - shift[i])
        dkh = grad(11)
        dth = grad(21)
        emit(
            11,
            adv(dkh)
            - lapse_lap
            + lapse * (aa + ktot * third)
            + FOUR_PI * lapse * (strace + dens)
            + 0.02 * lapse * theta,
        )
        src = sym(
            [
                -lcov[i][j] + lapse * (ricci[i][j] - (2.0 * FOUR_PI) * stress[i][j])
                for i, j in PAIRS
            ]
        )
        strc = trace(inv, src) * (1.0 / 3.0)
        for i, j in PAIRS:
            s = slot(i, j)
            acc = adv(dg[i][j])
            for k in R3:
                acc = acc + metric[i][k] * dsh[k][j] + metric[j][k] * dsh[k][i]
            emit(1 + s, acc - metric[i][j] * div23 - 2.0 * lapse * trl[i][j])
            prod = dot3(trl[i], [mixed[k][j] for k in R3])
            acc = adv(grad(12 + s))
            for k in R3:
                acc = acc + trl[i][k] * dsh[k][j] + trl[j][k] * dsh[k][i]
            emit(
                12 + s,
                acc
                - trl[i][j] * div23
                + chi * (src[i][j] - metric[i][j] * strc)
                + lapse * (ktot * trl[i][j] - 2.0 * prod),
            )
        hsh = [hess(8 + i) for i in R3]
        ddiv = [hsh[0][0][j] + hsh[1][1][j] + hsh[2][2][j] for j in R3]
        for i in R3:
            br = trace(up, raised[i])
            br = br - 1.5 * ichi * dot3(up[i], dchi)
            br = br - (1.0 / 3.0) * dot3(inv[i], [2.0 * dkh[j] + dth[j] for j in R3])
            br = br - (2.0 * FOUR_PI) * dot3(inv[i], mom)
            emit(
                18 + i,
                adv(dgam[i])
                - dot3(gd, dsh[i])
                + gd[i] * div23
                + trace(inv, hsh[i])
                + (1.0 / 3.0) * dot3(inv[i], ddiv)
                - 2.0 * dot3(up[i], dal)
                + 2.0 * lapse * br
                - 0.04 * lapse * (conn[i] - gd[i]),
            )
        emit(
            21,
            adv(dth)
            + 0.5
            * lapse
            * (rscal - aa + (2.0 / 3.0) * ktot * ktot - (4.0 * FOUR_PI) * dens)
            - 0.04 * lapse * theta,
        )
        return carry

    lax.fori_loop(0, 2, body, 0)


def compute_scratch():
    V = lambda *s: pltpu.VMEM(s, jnp.float32)
    return [
        V(10 * 3 * 16 * 8, 128),
        V(8, 80, 128),
        V(8, 64, 128),
        V(3, 80, 128),
        V(3, 64, 128),
        V(10, 48, 128),
        V(8, 48, 128),
        V(5, 48, 128),
    ]


def rates(T, scratch, o_st, o_fl, RT):
    G, PR, PH, EC, EH, FX, HR, EZ = scratch
    prim_stage(T, PR, PH, EC, EH)
    flux_stage(T, PR, PH, FX, HR)
    field_stage(EC, EH, EZ, HR)
    deriv_stage(T, G)
    algebra_stage(G, PR, HR, o_st, o_fl, RT)


MESH = pl.DeviceIdType.MESH
N_SLOTS = 29


def wave_stage(own):
    metric = sym([own(8 + v) for v in range(1, 7)])
    inv = inverse(metric)
    scale = 2.0 * own(8 + 7) * own(8)
    speeds = [jnp.abs(own(16 + d)) + jnp.sqrt(scale * inv[d][d]) for d in range(3)]
    return jnp.maximum(jnp.maximum(speeds[0], speeds[1]), speeds[2])


def load_stage(st, fl, o_st, o_fl, T):
    for u in range(30):
        src, dst, v = (fl, o_fl, u) if u < 8 else (st, o_st, u - 8)
        for x in range(4):
            value = src[v, x]
            T[pl.ds(row_of(u // 8, x + 3, 4) + u % 8, 4, stride=8), :] = value
            dst[v, pl.ds(4 * x, 4), :] = value


def local_stage(o_st, o_fl, zsend, mine):
    lane = lanes()

    def body(h, top):
        at = pl.ds(pl.multiple_of(8 * h, 8), 8)

        def own(u):
            return o_fl[u, at, :] if u < 8 else o_st[u - 8, at, :]

        last = jnp.zeros((8, 128), jnp.float32)
        first = jnp.zeros((8, 128), jnp.float32)
        for u in range(30):
            p = PACK - 3 * u
            here = (lane >= p) & (lane < p + 3)
            value = own(u)
            first = jnp.where(here, lroll(value, p), first)
            last = jnp.where(here, lroll(value, p - 125), last)
        zsend[0, at, :] = last
        zsend[1, at, :] = first
        return jnp.maximum(top, wave_stage(own))

    top = lax.fori_loop(0, 2, body, jnp.zeros((8, 128), jnp.float32))
    mine[0] = jnp.max(top, axis=0, keepdims=True)


def halo_rows(zrecv, T):
    for side in range(2):
        for x in range(4):
            T[pl.ds(row_of(3, x + 3, 4) + 6 + side, 4, stride=8), :] = zrecv[
                side, pl.ds(4 * x, 4), :
            ]


def kernel(st, fl, o_st, o_fl, T5, zsend, zrecv, mine, slots, RT, ssem, rsem, msem, *scratch):
    gx, gy, gz = lax.axis_index("gx"), lax.axis_index("gy"), lax.axis_index("gz")
    hi = gy % 2
    T = T5.reshape(3840, 128)

    def at_x(step):
        x2 = (hi * 4 + gz + step) % 8
        return (gx, gy - hi + x2 // 4, x2 % 4)

    ring_x = [at_x(k) for k in range(1, 8)]
    ring_y = [(gx, (gy + 2 * k) % 16, gz) for k in range(1, 8)]
    ring_z = [((gx + k) % 16, gy, gz) for k in range(1, 16)]
    x_up, x_dn = ((gx + 1) % 16, gy, gz), ((gx + 15) % 16, gy, gz)
    z_up, z_dn = (gx, gy, (gz + 1) % 4), (gx, gy, (gz + 3) % 4)
    partner = at_x(4)
    onward = (gx, (gy + 2 - 4 * hi + 16) % 16, gz)

    barrier = pltpu.get_barrier_semaphore()
    for peer in ring_x + ring_y + ring_z:
        pl.semaphore_signal(barrier, inc=1, device_id=peer, device_id_type=MESH)
    load_stage(st, fl, o_st, o_fl, T)
    local_stage(o_st, o_fl, zsend, mine)
    pl.semaphore_wait(barrier, N_SLOTS)

    started = []

    def send(src, dst, peer):
        k = len(started)
        copy = pltpu.make_async_remote_copy(
            src_ref=src,
            dst_ref=dst,
            send_sem=ssem.at[k],
            recv_sem=rsem.at[k],
            device_id=peer,
            device_id_type=MESH,
        )
        copy.start()
        started.append(copy)
        return copy

    def share(phase, base, peers):
        for k, peer in enumerate(peers):
            pltpu.make_async_remote_copy(
                src_ref=mine.at[phase],
                dst_ref=slots.at[base + k],
                send_sem=msem.at[phase],
                recv_sem=msem.at[3 + phase],
                device_id=peer,
                device_id_type=MESH,
            ).start()

    def gathered(phase, base, count):
        part = slots.at[pl.ds(base, count)]
        pltpu.make_async_copy(part, part, msem.at[3 + phase]).wait()
        mine[phase + 1] = jnp.maximum(mine[phase], jnp.max(slots[pl.ds(base, count)], axis=0))

    def drained(phase, base, count):
        part = slots.at[pl.ds(base, count)]
        pltpu.make_async_copy(part, part, msem.at[phase]).wait()

    def block(t, n, xp, nx, yp, ny):
        return T5.at[pl.ds(t, n), pl.ds(xp, nx), pl.ds(yp, ny)]

    def to_partner(t):
        return send(block(t, 1, 3, 4, 4, 4), block(t, 1, 3, 4, 8 * hi, 4), partner)

    def go_on(t):
        return send(block(t, 1, 3, 4, 9 - 9 * hi, 3), block(t, 1, 3, 4, 1 + 7 * hi, 3), onward)

    def faces(t, n):
        return [
            send(block(t, n, 3, 3, 4, 4), block(t, n, 7, 3, 4, 4), x_dn),
            send(block(t, n, 4, 3, 4, 4), block(t, n, 0, 3, 4, 4), x_up),
        ]

    def edges(t, n):
        copies = []
        for yp in (2, 8):
            copies.append(send(block(t, n, 3, 2, yp, 2), block(t, n, 7, 2, yp, 2), x_dn))
            copies.append(send(block(t, n, 5, 2, yp, 2), block(t, n, 1, 2, yp, 2), x_up))
        return copies

    zs = [send(zsend.at[0], zrecv.at[0], z_up), send(zsend.at[1], zrecv.at[1], z_dn)]
    share(0, 0, ring_x)
    far = [to_partner(t) for t in range(3)]
    side = faces(0, 3)
    for copy in zs:
        copy.wait_recv()
    halo_rows(zrecv, T)
    far.append(to_partner(3))
    side += faces(3, 1)
    gathered(0, 0, 7)
    share(1, 7, ring_y)
    relay = []
    for t in range(2):
        far[t].wait_recv()
        relay.append(go_on(t))
    gathered(1, 7, 7)
    share(2, 14, ring_z)
    for t in range(2, 4):
        far[t].wait_recv()
        relay.append(go_on(t))
    for t in range(2):
        relay[t].wait_recv()
    side += edges(0, 2)
    for t in range(2, 4):
        relay[t].wait_recv()
    side += edges(2, 2)
    for copy in side:
        copy.wait_recv()

    rates(T, scratch, o_st, o_fl, RT)
    gathered(2, 14, 15)
    step = 0.25 / jnp.max(mine[3], axis=1, keepdims=True)
    for v in range(22):
        o_st[v] = o_st[v] + step * RT[v]
    for v in range(8):
        o_fl[v] = o_fl[v] + step * RT[22 + v]
    for copy in started:
        copy.wait_send()
    drained(0, 0, 7)
    drained(1, 7, 7)
    drained(2, 14, 15)


N_COPIES = 2 + 8 + 4 + 8


def per_device(spacetime, fluid):
    vmem = pl.BlockSpec(memory_space=pltpu.VMEM)
    space = lambda *s: pltpu.VMEM(s, jnp.float32)
    st_new, fl_new = pl.pallas_call(
        kernel,
        out_shape=(
            jax.ShapeDtypeStruct((22, 16, 128), jnp.float32),
            jax.ShapeDtypeStruct((8, 16, 128), jnp.float32),
        ),
        in_specs=[vmem, vmem],
        out_specs=(vmem, vmem),
        scratch_shapes=[
            space(4, PADX, PADY, 8, 128),
            space(2, 16, 128),
            space(2, 16, 128),
            space(4, 1, 128),
            space(N_SLOTS, 1, 128),
            space(30, 16, 128),
            pltpu.SemaphoreType.DMA((30,)),
            pltpu.SemaphoreType.DMA((30,)),
            pltpu.SemaphoreType.DMA((6,)),
        ]
        + compute_scratch(),
        compiler_params=pltpu.CompilerParams(collective_id=1, has_side_effects=True),
    )(spacetime, fluid)
    return st_new.reshape(22, 4, 4, 128), fl_new.reshape(8, 4, 4, 128)


def solution(mesh):
    spec = P(None, "gx", "gy", "gz")
    return jax.shard_map(
        per_device, mesh=mesh, in_specs=(spec, spec), out_specs=(spec, spec), check_vma=False
    )
```

```python
import math
import jax
import jax.numpy as jnp
from jax import lax
from jax.experimental import pallas as pl
from jax.experimental.pallas import tpu as pltpu
from jax.sharding import PartitionSpec as P

RECOVERY_STEPS = 4
PAIRS = ((0, 0), (0, 1), (0, 2), (1, 1), (1, 2), (2, 2))
FOUR_PI = 4.0 * math.pi
PACK = 93
Z_TILE = 2
PADX, PADY = 10, 12
PLACE = (
    [(1, s) for s in range(8)]
    + [(2, 0), (2, 1), (2, 2)]
    + [(3, s) for s in range(7)]
    + [(2, 3), (2, 4), (2, 5), (3, 7)]
)


def slot(i, j):
    return PAIRS.index((min(i, j), max(i, j)))


def aligned(start):
    return pl.ds(start if isinstance(start, int) else pl.multiple_of(start, 8), 8)


def row_of(t, xp, yp):
    return ((t * PADX + xp) * PADY + yp) * 8


def lanes():
    return lax.broadcasted_iota(jnp.int32, (8, 128), 1)


def rows_iota():
    return lax.broadcasted_iota(jnp.int32, (8, 128), 0)


def lroll(v, amount):
    amount = amount % 128
    return v if amount == 0 else pltpu.roll(v, amount, 1)


def shifted(f, halo, k, lane):
    if k > 0:
        return lroll(jnp.where(lane < k, halo, f), 128 - k)
    return lroll(jnp.where(lane >= 128 + k, halo, f), -k)


def d_one(m2, m1, p1, p2):
    return (8.0 / 12.0) * (p1 - m1) - (1.0 / 12.0) * (p2 - m2)


def line_derivs(v, second):
    s1 = v[1] + v[-1]
    s2 = v[2] + v[-2]
    s3 = v[3] + v[-3]
    first = (8.0 / 12.0) * (v[1] - v[-1]) - (1.0 / 12.0) * (v[2] - v[-2])
    kreiss = (0.2 / 64.0) * s3 - (0.2 * 6.0 / 64.0) * s2 + (0.2 * 15.0 / 64.0) * s1
    sec = None
    if second:
        sec = (16.0 / 12.0) * s1 - (1.0 / 12.0) * s2 - (30.0 / 12.0) * v[0]
    return first, kreiss, sec


def fanned(v, amount):
    if amount + 21 >= 128:
        v, amount = lroll(v, amount), 0
    return pltpu.roll(v, amount, 1, stride=3, stride_axis=0)


def expand(lo, hi, t, lane):
    up = fanned(hi, 128 - PACK + 24 * t)
    dn = fanned(lo, 125 - PACK + 24 * t)
    return jnp.where(lane < 3, up, dn)


def tile_at(T, t, xp, yp):
    return T[aligned(row_of(t, xp, yp)), :]


def packed_at(T, xp, yp):
    base = row_of(Z_TILE, xp, yp)
    return [jnp.broadcast_to(T[pl.ds(base + 6 + side, 1), :], (8, 128)) for side in range(2)]


def deriv_at(q, t, xy):
    return aligned(((q * 3 + t - 1) * 16 + xy) * 8)


NEAR = (-2, -1, 1, 2)


def by_four(column):
    def body(x, carry):
        for y in range(4):
            column(4 * x + y)
        return carry

    lax.fori_loop(0, 4, body, 0)


def deriv_xz(T, G, tiles):
    lane = lanes()

    def column(xy):
        xp, yp = xy // 4 + 3, xy % 4 + 4
        own = packed_at(T, xp, yp)
        around = [packed_at(T, xp + a, yp) for a in NEAR]
        border = [d_one(*[around[i][side] for i in range(4)]) for side in range(2)]
        for t in tiles:
            second = t < 3
            vx = {a: tile_at(T, t, xp + a, yp) for a in range(-3, 4)}
            halo = expand(own[0], own[1], t, lane)
            vz = {a: shifted(vx[0], halo, a, lane) if a else vx[0] for a in range(-3, 4)}
            dx, kx, sx = line_derivs(vx, second)
            dz, kz, sz = line_derivs(vz, second)
            G[deriv_at(0, t, xy), :] = dx
            G[deriv_at(2, t, xy), :] = dz
            G[deriv_at(3, t, xy), :] = kx + kz - (0.2 * 60.0 / 64.0) * vx[0]
            if second:
                cross = expand(border[0], border[1], t, lane)
                G[deriv_at(4, t, xy), :] = sx
                G[deriv_at(6, t, xy), :] = d_one(*[shifted(dx, cross, a, lane) for a in NEAR])
                G[deriv_at(9, t, xy), :] = sz

    by_four(column)


def deriv_y(T, G, tiles):
    lane = lanes()

    def column(xy):
        xp, yp = xy // 4 + 3, xy % 4 + 4
        around = [packed_at(T, xp, yp + a) for a in NEAR]
        border = [d_one(*[around[i][side] for i in range(4)]) for side in range(2)]
        for t in tiles:
            second = t < 3
            vy = {a: tile_at(T, t, xp, yp + a) for a in range(-3, 4)}
            dy, ky, sy = line_derivs(vy, second)
            G[deriv_at(1, t, xy), :] = dy
            G[deriv_at(3, t, xy), :] = G[deriv_at(3, t, xy), :] + ky
            if second:
                cross = expand(border[0], border[1], t, lane)
                G[deriv_at(7, t, xy), :] = sy
                G[deriv_at(8, t, xy), :] = d_one(*[shifted(dy, cross, a, lane) for a in NEAR])

    by_four(column)


def deriv_xy(T, G, tiles):
    def column(xy):
        xp, yp = xy // 4 + 3, xy % 4 + 4
        for t in tiles:
            rows = [d_one(*[tile_at(T, t, xp + a, yp + b) for b in NEAR]) for a in NEAR]
            G[deriv_at(5, t, xy), :] = d_one(*rows)

    by_four(column)


def dot3(a, b):
    return a[0] * b[0] + a[1] * b[1] + a[2] * b[2]


def recover(cons, mag):
    density = cons[0]
    mom = cons[1:4]
    energy = cons[4] + density
    mom_sq = dot3(mom, mom)
    mag_sq = dot3(mag, mag)
    cross = dot3(mom, mag)
    cross_sq = cross * cross

    def state(z):
        zb = z + mag_sq
        zz = z * z
        speed_sq = (mom_sq * zz + cross_sq * (2.0 * z + mag_sq)) / (zz * zb * zb)
        ilsq = 1.0 - jnp.minimum(speed_sq, 0.99)
        rho = density * jnp.sqrt(ilsq)
        return ilsq, rho, 0.5 * (z * ilsq - rho)

    z = jnp.maximum(energy - 0.5 * mag_sq, density)
    for _ in range(RECOVERY_STEPS):
        ilsq, rho, p = state(z)
        res = z + mag_sq - p - 0.5 * mag_sq * ilsq - 0.5 * cross_sq / (z * z) - energy
        z = jnp.maximum(z - res / (1.0 - 0.5 * ilsq), density)
    ilsq, rho, p = state(z)
    p = jnp.maximum(p, 0.01 * rho)
    lor = 1.0 / jnp.sqrt(ilsq)
    factor = lor / (z + mag_sq)
    cz = cross / z
    return rho, p, [factor * (mom[i] + cz * mag[i]) for i in range(3)]


def prim_stage(T, PR, PH, EC, EH, columns, halo_columns):
    lane = lanes()

    def strip(t, s, xp, dy=0):
        return T[pl.ds(row_of(t, xp + 1, 2 + dy) + s, 8, stride=8), :]

    def finish(cons, low, up, chi, lapse):
        root = chi * jnp.sqrt(chi)
        centred = [0.5 * (low[i] + up[i]) for i in range(3)]
        mag = [c * root for c in centred]
        rho, p, u = recover([c * root for c in cons], mag)
        inv = -lapse / jnp.sqrt(1.0 + dot3(u, u))
        vel = [a * inv for a in u]
        ele = [
            vel[(i + 1) % 3] * centred[(i + 2) % 3] - vel[(i + 2) % 3] * centred[(i + 1) % 3]
            for i in range(3)
        ]
        return [rho, p] + u + mag, ele

    def body(xp):
        own = [strip(0, s, xp) for s in range(8)]
        zhi = strip(Z_TILE, 7, xp)
        upper = [
            strip(0, 5, xp + 1),
            strip(0, 6, xp, 1),
            jnp.where(lane == 127, lroll(zhi, 127 - (PACK - 21)), lroll(own[7], 127)),
        ]
        prims, ele = finish(own[:5], own[5:], upper, strip(1, 0, xp), strip(1, 7, xp))
        at = aligned(8 + xp * 8)
        for q in range(8):
            PR[q, at, :] = prims[q]
        for i in range(3):
            EC[i, at, :] = ele[i]

    for xp in columns:
        body(xp)

    def body_h(k):
        xp = k + 1

        def halo(u, xq, dy=0):
            p = PACK - 3 * u
            return jnp.where(
                lane < 3, lroll(strip(Z_TILE, 7, xq, dy), -p), lroll(strip(Z_TILE, 6, xq, dy), 125 - p)
            )

        vals = [halo(u, xp) for u in range(9)]
        inner = T[pl.ds(row_of(0, xp + 1, 2) + 7, 8, stride=8), :]
        upper = [
            halo(5, xp + 1),
            halo(6, xp, 1),
            lroll(jnp.where(lane == 0, inner, vals[7]), 127),
        ]
        prims, ele = finish(vals[:5], vals[5:8], upper, vals[8], halo(15, xp))
        at = aligned(8 + k * 8)
        for q in range(8):
            PH[q, at, :] = prims[q]
        for i in range(3):
            EH[i, at, :] = ele[i]

    for k in halo_columns:
        body_h(k)


def limited(a, b):
    return jnp.maximum(jnp.minimum(a, b), 0.0) + jnp.minimum(jnp.maximum(a, b), 0.0)


def stress_parts(rho, p, u, mag):
    lor_sq = 1.0 + dot3(u, u)
    lor = jnp.sqrt(lor_sq)
    inv = 1.0 / lor
    vel = [a * inv for a in u]
    along = dot3(vel, mag)
    b0 = lor * along
    b = [mag[i] * inv + b0 * vel[i] for i in range(3)]
    bsq = dot3(mag, mag) * (inv * inv) + along * along
    enth = rho + 2.0 * p
    inertia = enth + bsq
    return lor, lor_sq, vel, b0, b, bsq, enth, inertia, p + 0.5 * bsq


def face_state(rho, p, u, mag, d):
    lor, lor_sq, vel, b0, b, bsq, enth, inertia, ptot = stress_parts(rho, p, u, mag)
    dens = rho * lor
    wl = inertia * lor_sq
    mom = [wl * vel[j] - b0 * b[j] for j in range(3)]
    cons = [dens] + mom + [wl - ptot - b0 * b0 - dens]
    wv = wl * vel[d]
    flux = [dens * vel[d]]
    for j in range(3):
        f = wv * vel[j] - b[d] * b[j]
        flux.append(f + ptot if j == d else f)
    flux.append(mom[d] - dens * vel[d])
    vsq = dot3(vel, vel)
    cs = 2.0 * p / enth
    va = bsq / inertia
    a2 = cs + va - cs * va
    vd = vel[d]
    spread = jnp.sqrt(a2 * (1.0 - vsq) * (1.0 - vsq * a2 - vd * vd * (1.0 - a2)))
    mid = vd * (1.0 - a2)
    fast = jnp.maximum(jnp.abs(mid + spread), jnp.abs(mid - spread)) / (1.0 - vsq * a2)
    return cons, flux, fast


def face_flux(left, right, normal, chi, lapse, d):
    root = chi * jnp.sqrt(chi)
    states = []
    for side in (left, right):
        mag = list(side[5:8])
        mag[d] = normal * root
        states.append(face_state(side[0], side[1], side[2:5], mag, d))
    (cl, fl, sl), (cr, fr, sr) = states
    sig = jnp.maximum(sl, sr)
    weight = 0.5 * lapse / root
    return [weight * (fl[q] + fr[q] - sig * (cr[q] - cl[q])) for q in range(5)]


def recon(m2, m1, c0, p1):
    mid = c0 - m1
    return m1 + 0.5 * limited(m1 - m2, mid), c0 - 0.5 * limited(mid, p1 - c0)


def flux_stage(T, PR, PH, FX, HR):
    lane = lanes()

    def strip(t, s, x, dy=0):
        return T[pl.ds(row_of(t, x + 3, 2 + dy) + s, 8, stride=8), :]

    def prim(q, x, dy=0):
        return PR[q, pl.ds(8 + (x + 2) * 8 + dy, 8), :]

    def half(a, b):
        return 0.5 * (a + b)

    def body_x(i):
        both = [recon(*[prim(q, i + a) for a in (-2, -1, 0, 1)]) for q in range(8)]
        chi = half(strip(1, 0, i - 1), strip(1, 0, i))
        lapse = half(strip(1, 7, i - 1), strip(1, 7, i))
        out = face_flux([b[0] for b in both], [b[1] for b in both], strip(0, 5, i), chi, lapse, 0)
        at = aligned(i * 8)
        for q in range(5):
            FX[q, at, :] = out[q]

    for i in range(5):
        body_x(i)

    def body(x):
        at = aligned(x * 8)
        up = aligned(x * 8 + 8)
        chi0, lapse0 = strip(1, 0, x), strip(1, 7, x)
        both = [recon(*[prim(q, x, a) for a in (-2, -1, 0, 1)]) for q in range(8)]
        chi = half(strip(1, 0, x, -1), chi0)
        lapse = half(strip(1, 7, x, -1), lapse0)
        fy = face_flux([b[0] for b in both], [b[1] for b in both], strip(0, 6, x), chi, lapse, 1)
        zlo, zhi = strip(Z_TILE, 6, x), strip(Z_TILE, 7, x)

        def halo(u):
            p = PACK - 3 * u
            return jnp.where(lane < 3, lroll(zhi, -p), lroll(zlo, 125 - p))

        chih, lapseh = halo(8), halo(15)
        own = [prim(q, x) for q in range(8)]
        hal = [PH[q, aligned(8 + (x + 1) * 8), :] for q in range(8)]
        both = [
            recon(
                shifted(own[q], hal[q], -2, lane),
                shifted(own[q], hal[q], -1, lane),
                own[q],
                shifted(own[q], hal[q], 1, lane),
            )
            for q in range(8)
        ]
        bz = strip(0, 7, x)
        fz = face_flux(
            [b[0] for b in both],
            [b[1] for b in both],
            bz,
            half(shifted(chi0, chih, -1, lane), chi0),
            half(shifted(lapse0, lapseh, -1, lane), lapse0),
            2,
        )
        both = [
            recon(lroll(own[q], 2), lroll(own[q], 1), hal[q], lroll(hal[q], 127)) for q in range(8)
        ]
        fl = face_flux(
            [b[0] for b in both],
            [b[1] for b in both],
            halo(7),
            half(lroll(chi0, 1), chih),
            half(lroll(lapse0, 1), lapseh),
            2,
        )
        for q in range(5):
            FX[5 + q, at, :] = fy[q]
        for q in range(5):
            fzu = lroll(jnp.where(lane == 0, fl[q], fz[q]), 127)
            fyu = FX[5 + q, pl.ds(x * 8 + 1, 8), :]
            HR[q, at, :] = (fz[q] - fzu) + (fy[q] - fyu) + (FX[q, at, :] - FX[q, up, :])

    for x in range(4):
        body(x)


def field_stage(EC, EH, EZ, HR):
    lane = lanes()

    def ec(i, x, dy=0):
        return EC[i, pl.ds(8 + (x + 2) * 8 + dy, 8), :]

    def eh(i, x, dy=0):
        return EH[i, pl.ds(8 + (x + 1) * 8 + dy, 8), :]

    for x in range(5):
        at = pl.ds(x * 8, 8)
        EZ[0, at, :] = 0.25 * (ec(2, x - 1, -1) + ec(2, x, -1) + ec(2, x - 1) + ec(2, x))
        s = ec(1, x - 1) + ec(1, x)
        h = eh(1, x - 1) + eh(1, x)
        EZ[1, at, :] = 0.25 * (shifted(s, h, -1, lane) + s)
        EZ[2, at, :] = 0.25 * (shifted(s, h, 1, lane) + s)
        if x < 4:
            s = ec(0, x, -1) + ec(0, x)
            h = eh(0, x, -1) + eh(0, x)
            EZ[3, at, :] = 0.25 * (shifted(s, h, -1, lane) + s)
            EZ[4, at, :] = 0.25 * (shifted(s, h, 1, lane) + s)
    for x in range(4):
        at, up, yu = pl.ds(x * 8, 8), pl.ds(x * 8 + 8, 8), pl.ds(x * 8 + 1, 8)
        ez = EZ[0, at, :]
        HR[5, at, :] = (EZ[2, at, :] - EZ[1, at, :]) - (EZ[0, yu, :] - ez)
        HR[6, at, :] = (EZ[0, up, :] - ez) - (EZ[4, at, :] - EZ[3, at, :])
        HR[7, at, :] = (EZ[3, yu, :] - EZ[3, at, :]) - (EZ[1, up, :] - EZ[1, at, :])


def sym(values):
    return [[values[slot(i, j)] for j in range(3)] for i in range(3)]


def trace(inv, m):
    return (
        inv[0][0] * m[0][0]
        + inv[1][1] * m[1][1]
        + inv[2][2] * m[2][2]
        + 2.0 * (inv[0][1] * m[0][1] + inv[0][2] * m[0][2] + inv[1][2] * m[1][2])
    )


def inverse(g):
    c00 = g[1][1] * g[2][2] - g[1][2] * g[1][2]
    c01 = g[0][2] * g[1][2] - g[0][1] * g[2][2]
    c02 = g[0][1] * g[1][2] - g[0][2] * g[1][1]
    c11 = g[0][0] * g[2][2] - g[0][2] * g[0][2]
    c12 = g[0][1] * g[0][2] - g[0][0] * g[1][2]
    c22 = g[0][0] * g[1][1] - g[0][1] * g[0][1]
    r = 1.0 / (g[0][0] * c00 + g[0][1] * c01 + g[0][2] * c02)
    return sym([c00 * r, c01 * r, c02 * r, c11 * r, c12 * r, c22 * r])


R3 = range(3)


def algebra_stage(G, PR, HR, o_st, o_fl, RT):
    low = rows_iota() < 4

    def body(h, carry):
        x = 2 * h

        def fold(a, b):
            return jnp.where(low, a, b)

        at = aligned(8 * h)

        def strip(ref, q, pad):
            return fold(
                ref[q, pl.ds(pad + x * 8 + 2, 8), :], ref[q, pl.ds(pad + x * 8 + 8 - 2, 8), :]
            )

        def g(q, v):
            t, s = PLACE[v]
            return G[pl.ds(((q * 3 + t - 1) * 16 + 8 * h) * 8 + s, 8, stride=8), :]

        cur = [o_st[v, at, :] for v in range(22)]
        flu = [o_fl[v, at, :] for v in range(8)]
        prims = [strip(PR, q, 8 + 16) for q in range(8)]

        def grad(v):
            return [g(k, v) for k in R3]

        def hess(v):
            return sym([g(4 + s, v) for s in range(6)])

        chi, lapse = cur[0], cur[7]
        metric = sym(cur[1:7])
        shift = cur[8:11]
        khat, theta = cur[11], cur[21]
        trl = sym(cur[12:18])
        conn = cur[18:21]
        inv = inverse(metric)
        ichi = 1.0 / chi
        root = chi * jnp.sqrt(chi)
        ktot = khat + 2.0 * theta

        lor, lor_sq, vel, b0, b, bsq, enth, inertia, ptot = stress_parts(
            prims[0], prims[1], prims[2:5], prims[5:8]
        )
        wl = inertia * lor_sq
        stress = sym(
            [
                wl * vel[i] * vel[j] - b[i] * b[j] + (ptot if i == j else 0.0)
                for i, j in PAIRS
            ]
        )
        total = flu[4] + flu[0]
        dens = total * root
        mom = [flu[1 + i] * root for i in R3]
        dal = grad(7)
        dsh = [grad(8 + i) for i in R3]
        hydro = [strip(HR, q, 0) for q in range(8)]
        for i in R3:
            hydro[1 + i] = (
                hydro[1 + i]
                - total * dal[i]
                + (flu[1] * dsh[0][i] + flu[2] * dsh[1][i] + flu[3] * dsh[2][i])
            )
        third = ktot * (1.0 / 3.0)
        curv = sym([(trl[i][j] + metric[i][j] * third) * ichi for i, j in PAIRS])
        tk = (
            stress[0][0] * curv[0][0]
            + stress[1][1] * curv[1][1]
            + stress[2][2] * curv[2][2]
            + 2.0
            * (stress[0][1] * curv[0][1] + stress[0][2] * curv[0][2] + stress[1][2] * curv[1][2])
        )
        hydro[4] = hydro[4] + lapse / root * tk - dot3(flu[1:4], dal)
        for q in range(8):
            RT[22 + q, at, :] = hydro[q]

        def adv(gr):
            return shift[0] * gr[0] + shift[1] * gr[1] + shift[2] * gr[2]

        def emit(v, rate):
            RT[v, at, :] = rate + g(3, v)

        dg = [[grad(1 + slot(i, j)) if i <= j else None for j in R3] for i in R3]
        dg = [[dg[min(i, j)][max(i, j)] for j in R3] for i in R3]
        lowered = [
            sym([0.5 * (dg[i][k][j] + dg[i][j][k] - dg[j][k][i]) for j, k in PAIRS]) for i in R3
        ]
        raised = [
            sym(
                [
                    inv[i][0] * lowered[0][j][k]
                    + inv[i][1] * lowered[1][j][k]
                    + inv[i][2] * lowered[2][j][k]
                    for j, k in PAIRS
                ]
            )
            for i in R3
        ]
        gd = [trace(inv, raised[i]) for i in R3]
        dchi = grad(0)
        hchi = hess(0)
        xcov = sym(
            [hchi[i][j] - dot3([raised[k][i][j] for k in R3], dchi) for i, j in PAIRS]
        )
        chi_lap = trace(inv, xcov)
        uchi = [dot3(inv[i], dchi) for i in R3]
        chi_sq = dot3(uchi, dchi)
        cross = dot3(uchi, dal)
        hal = hess(7)
        half_ichi = 0.5 * ichi
        lcov = sym(
            [
                hal[i][j]
                - dot3([raised[k][i][j] for k in R3], dal)
                + (dchi[i] * dal[j] + dchi[j] * dal[i] - metric[i][j] * cross) * half_ichi
                for i, j in PAIRS
            ]
        )
        lapse_lap = chi * trace(inv, lcov)
        dgam = [grad(18 + i) for i in R3]
        cu = [
            [
                [
                    inv[l][0] * lowered[j][k][0]
                    + inv[l][1] * lowered[j][k][1]
                    + inv[l][2] * lowered[j][k][2]
                    for l in R3
                ]
                for k in R3
            ]
            for j in R3
        ]
        quarter = half_ichi * half_ichi
        ricci = []
        for i, j in PAIRS:
            v = 1 + slot(i, j)
            hg = hess(v)
            r = -0.5 * trace(inv, hg)
            for k in R3:
                r = r + 0.5 * (metric[k][i] * dgam[k][j] + metric[k][j] * dgam[k][i])
                r = r + 0.5 * gd[k] * (lowered[i][j][k] + lowered[j][i][k])
            for k in R3:
                for l in R3:
                    r = r + raised[k][l][i] * cu[j][k][l]
                    r = r + raised[k][l][j] * cu[i][k][l]
                    r = r + raised[k][i][l] * cu[k][j][l]
            r = r + (xcov[i][j] + metric[i][j] * chi_lap) * half_ichi
            r = r - (dchi[i] * dchi[j] + 3.0 * metric[i][j] * chi_sq) * quarter
            ricci.append(r)
        ricci = sym(ricci)
        rscal = chi * trace(inv, ricci)
        strace = chi * trace(inv, stress)
        mixed = [[dot3(inv[i], [trl[k][j] for k in R3]) for j in R3] for i in R3]
        up = sym([dot3(mixed[i], inv[j]) for i, j in PAIRS])
        aa = trace(trl, up)
        div = dsh[0][0] + dsh[1][1] + dsh[2][2]
        div23 = (2.0 / 3.0) * div

        emit(0, adv(dchi) + (2.0 / 3.0) * chi * (lapse * ktot - div))
        emit(7, adv(dal) - 2.0 * lapse * khat)
        for i in R3:
            emit(8 + i, adv(dsh[i]) + 0.75 * conn[i] - shift[i])
        dkh = grad(11)
        dth = grad(21)
        emit(
            11,
            adv(dkh)
            - lapse_lap
            + lapse * (aa + ktot * third)
            + FOUR_PI * lapse * (strace + dens)
            + 0.02 * lapse * theta,
        )
        src = sym(
            [
                -lcov[i][j] + lapse * (ricci[i][j] - (2.0 * FOUR_PI) * stress[i][j])
                for i, j in PAIRS
            ]
        )
        strc = trace(inv, src) * (1.0 / 3.0)
        for i, j in PAIRS:
            s = slot(i, j)
            acc = adv(dg[i][j])
            for k in R3:
                acc = acc + metric[i][k] * dsh[k][j] + metric[j][k] * dsh[k][i]
            emit(1 + s, acc - metric[i][j] * div23 - 2.0 * lapse * trl[i][j])
            prod = dot3(trl[i], [mixed[k][j] for k in R3])
            acc = adv(grad(12 + s))
            for k in R3:
                acc = acc + trl[i][k] * dsh[k][j] + trl[j][k] * dsh[k][i]
            emit(
                12 + s,
                acc
                - trl[i][j] * div23
                + chi * (src[i][j] - metric[i][j] * strc)
                + lapse * (ktot * trl[i][j] - 2.0 * prod),
            )
        hsh = [hess(8 + i) for i in R3]
        ddiv = [hsh[0][0][j] + hsh[1][1][j] + hsh[2][2][j] for j in R3]
        for i in R3:
            br = trace(up, raised[i])
            br = br - 1.5 * ichi * dot3(up[i], dchi)
            br = br - (1.0 / 3.0) * dot3(inv[i], [2.0 * dkh[j] + dth[j] for j in R3])
            br = br - (2.0 * FOUR_PI) * dot3(inv[i], mom)
            emit(
                18 + i,
                adv(dgam[i])
                - dot3(gd, dsh[i])
                + gd[i] * div23
                + trace(inv, hsh[i])
                + (1.0 / 3.0) * dot3(inv[i], ddiv)
                - 2.0 * dot3(up[i], dal)
                + 2.0 * lapse * br
                - 0.04 * lapse * (conn[i] - gd[i]),
            )
        emit(
            21,
            adv(dth)
            + 0.5
            * lapse
            * (rscal - aa + (2.0 / 3.0) * ktot * ktot - (4.0 * FOUR_PI) * dens)
            - 0.04 * lapse * theta,
        )
        return carry

    lax.fori_loop(0, 2, body, 0)


def compute_scratch():
    V = lambda *s: pltpu.VMEM(s, jnp.float32)
    return [
        V(10 * 3 * 16 * 8, 128),
        V(8, 80, 128),
        V(8, 64, 128),
        V(3, 80, 128),
        V(3, 64, 128),
        V(10, 48, 128),
        V(8, 48, 128),
        V(5, 48, 128),
    ]


MESH = pl.DeviceIdType.MESH
PHASES = ((0, 1), (1, 7), (8, 7), (15, 7))
N_SLOTS = 22
N_GREETED = 18


def wave_stage(own):
    metric = sym([own(8 + v) for v in range(1, 7)])
    inv = inverse(metric)
    scale = 2.0 * own(8 + 7) * own(8)
    speeds = [jnp.abs(own(16 + d)) + jnp.sqrt(scale * inv[d][d]) for d in range(3)]
    return jnp.maximum(jnp.maximum(speeds[0], speeds[1]), speeds[2])


def load_stage(st, fl, o_st, o_fl, T):
    for u in range(30):
        src, dst, v = (fl, o_fl, u) if u < 8 else (st, o_st, u - 8)
        t, s = (0, u) if u < 8 else PLACE[v]
        for x in range(4):
            value = src[v, x]
            T[pl.ds(row_of(t, x + 3, 4) + s, 4, stride=8), :] = value
            dst[v, pl.ds(4 * x, 4), :] = value


def speed_stage(st, mine):
    top = None
    for x in range(4):

        def own(u):
            return st[u - 8, x]

        speed = wave_stage(own)
        top = speed if top is None else jnp.maximum(top, speed)
    mine[0] = jnp.max(top, axis=0, keepdims=True)


def border_stage(o_st, o_fl, zsend):
    lane = lanes()

    def body(h, carry):
        at = pl.ds(pl.multiple_of(8 * h, 8), 8)
        last = jnp.zeros((8, 128), jnp.float32)
        first = jnp.zeros((8, 128), jnp.float32)
        for u in range(30):
            t, s = (0, u) if u < 8 else PLACE[u - 8]
            p = PACK - 3 * (8 * t + s)
            here = (lane >= p) & (lane < p + 3)
            value = o_fl[u, at, :] if u < 8 else o_st[u - 8, at, :]
            first = jnp.where(here, lroll(value, p), first)
            last = jnp.where(here, lroll(value, p - 125), last)
        zsend[0, at, :] = last
        zsend[1, at, :] = first
        return carry

    lax.fori_loop(0, 2, body, 0)


def halo_rows(zrecv, T):
    for side in range(2):
        for x in range(4):
            T[pl.ds(row_of(Z_TILE, x + 3, 4) + 6 + side, 4, stride=8), :] = zrecv[
                side, pl.ds(4 * x, 4), :
            ]


def kernel(st, fl, o_st, o_fl, T5, zsend, zrecv, mine, slots, RT, ssem, rsem, msem, known, *scratch):
    gx, gy, gz = lax.axis_index("gx"), lax.axis_index("gy"), lax.axis_index("gz")
    hi, core = gy & 1, gx & 1
    T = T5.reshape(3840, 128)

    def at_x(step):
        x2 = (hi * 4 + gz + step) & 7
        return (gx, gy - hi + (x2 >> 2), x2 & 3)

    mate = (gx + 1 - 2 * core, gy, gz)
    ring_x = [at_x(k) for k in range(1, 8)]
    ring_y = [(gx, (gy + 2 * k) & 15, gz) for k in range(1, 8)]
    ring_z = [((gx + 2 * k) & 15, gy, gz) for k in range(1, 8)]
    x_up, x_dn = ((gx + 1) & 15, gy, gz), ((gx + 15) & 15, gy, gz)
    z_up, z_dn = (gx, gy, (gz + 1) & 3), (gx, gy, (gz + 3) & 3)
    y_up, y_dn = ring_y[0], ring_y[6]
    cross = ((gx + 15 + 2 * core) & 15, gy, gz)
    partner = ring_x[3]
    onward = (gx, (gy + 2 - 4 * hi) & 15, gz)

    barrier = pltpu.get_barrier_semaphore()
    for peer in [partner, mate, cross, y_up, y_dn] + ring_x[:3] + ring_x[4:] + ring_z:
        pl.semaphore_signal(barrier, inc=1, device_id=peer, device_id_type=MESH)
    speed_stage(st, mine)
    load_stage(st, fl, o_st, o_fl, T)
    border_stage(o_st, o_fl, zsend)
    pl.semaphore_wait(barrier, N_GREETED)

    def tell(step):
        for peer in (y_up, y_dn):
            pl.semaphore_signal(known.at[step], inc=1, device_id=peer, device_id_type=MESH)

    def told(step):
        pl.semaphore_wait(known.at[step], 2)

    tell(0)
    started = []

    def send(src, dst, peer):
        k = len(started)
        copy = pltpu.make_async_remote_copy(
            src_ref=src,
            dst_ref=dst,
            send_sem=ssem.at[k],
            recv_sem=rsem.at[k],
            device_id=peer,
            device_id_type=MESH,
        )
        copy.start()
        started.append(copy)
        return copy

    def share(phase, peers):
        base = PHASES[phase][0]
        for k, peer in enumerate(peers):
            pltpu.make_async_remote_copy(
                src_ref=mine.at[phase],
                dst_ref=slots.at[base + k],
                send_sem=msem.at[phase],
                recv_sem=msem.at[4 + phase],
                device_id=peer,
                device_id_type=MESH,
            ).start()

    def gathered(phase):
        part = slots.at[pl.ds(*PHASES[phase])]
        pltpu.make_async_copy(part, part, msem.at[4 + phase]).wait()
        mine[phase + 1] = jnp.maximum(mine[phase], jnp.max(slots[pl.ds(*PHASES[phase])], axis=0))

    def drained(phase):
        part = slots.at[pl.ds(*PHASES[phase])]
        pltpu.make_async_copy(part, part, msem.at[phase]).wait()

    def block(t, n, xp, nx, yp, ny):
        return T5.at[pl.ds(t, n), pl.ds(xp, nx), pl.ds(yp, ny)]

    def to_partner(t):
        return send(block(t, 1, 3, 4, 4, 4), block(t, 1, 3, 4, 8 * hi, 4), partner)

    def go_on(t):
        return send(block(t, 1, 3, 4, 9 - 9 * hi, 3), block(t, 1, 3, 4, 1 + 7 * hi, 3), onward)

    def faces(t, n):
        return [
            send(block(t, n, 3, 3, 4, 4), block(t, n, 7, 3, 4, 4), x_dn),
            send(block(t, n, 4, 3, 4, 4), block(t, n, 0, 3, 4, 4), x_up),
        ]

    def edges(t, n):
        copies = []
        for yp in (2, 8):
            copies.append(send(block(t, n, 3, 2, yp, 2), block(t, n, 7, 2, yp, 2), x_dn))
            copies.append(send(block(t, n, 5, 2, yp, 2), block(t, n, 1, 2, yp, 2), x_up))
        return copies

    G, PR, PH, EC, EH, FX, HR, EZ = scratch
    far, relay, side = {}, {}, {}
    share(0, [mate])
    zs = [send(zsend.at[0], zrecv.at[0], z_up), send(zsend.at[1], zrecv.at[1], z_dn)]
    for t in range(2):
        far[t] = to_partner(t)
    front = faces(0, 2)
    gathered(0)
    share(1, ring_z)
    for copy in zs:
        copy.wait_recv()
    halo_rows(zrecv, T)
    for t in (2, 3):
        far[t] = to_partner(t)
    front += faces(2, 2)
    told(0)
    tell(1)
    for copy in front:
        copy.wait_recv()
    deriv_xz(T, G, (1,))
    far[0].wait_recv()
    relay[0] = go_on(0)
    gathered(1)
    share(2, ring_x)
    told(1)
    tell(2)
    deriv_xz(T, G, (2,))
    far[1].wait_recv()
    relay[1] = go_on(1)
    far[2].wait_recv()
    relay[2] = go_on(2)
    for t in range(2):
        relay[t].wait_recv()
        side[t] = edges(t, 1)
    gathered(2)
    told(2)
    share(3, ring_y)
    far[3].wait_recv()
    relay[3] = go_on(3)
    relay[2].wait_recv()
    side[2] = edges(2, 1)
    deriv_xz(T, G, (3,))
    prim_stage(T, PR, PH, EC, EH, (2, 3, 4), (1, 2, 3))
    deriv_y(T, G, (1, 2))
    relay[3].wait_recv()
    deriv_y(T, G, (3,))
    for t in range(3):
        for copy in side[t]:
            copy.wait_recv()
    deriv_xy(T, G, (1, 2))
    prim_stage(T, PR, PH, EC, EH, (0, 1, 5, 6, 7), (0, 4, 5))
    flux_stage(T, PR, PH, FX, HR)
    field_stage(EC, EH, EZ, HR)
    algebra_stage(G, PR, HR, o_st, o_fl, RT)
    gathered(3)
    step = 0.25 / jnp.max(mine[4], axis=1, keepdims=True)
    for v in range(22):
        o_st[v] = o_st[v] + step * RT[v]
    for v in range(8):
        o_fl[v] = o_fl[v] + step * RT[22 + v]
    for copy in started:
        copy.wait_send()
    for phase in range(4):
        drained(phase)


def per_device(spacetime, fluid):
    vmem = pl.BlockSpec(memory_space=pltpu.VMEM)
    space = lambda *s: pltpu.VMEM(s, jnp.float32)
    st_new, fl_new = pl.pallas_call(
        kernel,
        out_shape=(
            jax.ShapeDtypeStruct((22, 16, 128), jnp.float32),
            jax.ShapeDtypeStruct((8, 16, 128), jnp.float32),
        ),
        in_specs=[vmem, vmem],
        out_specs=(vmem, vmem),
        scratch_shapes=[
            space(4, PADX, PADY, 8, 128),
            space(2, 16, 128),
            space(2, 16, 128),
            space(5, 1, 128),
            space(N_SLOTS, 1, 128),
            space(30, 16, 128),
            pltpu.SemaphoreType.DMA((32,)),
            pltpu.SemaphoreType.DMA((32,)),
            pltpu.SemaphoreType.DMA((8,)),
            pltpu.SemaphoreType.REGULAR((3,)),
        ]
        + compute_scratch(),
        compiler_params=pltpu.CompilerParams(
            collective_id=1, has_side_effects=True, vmem_limit_bytes=16 << 20
        ),
    )(spacetime, fluid)
    return st_new.reshape(22, 4, 4, 128), fl_new.reshape(8, 4, 4, 128)


def solution(mesh):
    spec = P(None, "gx", "gy", "gz")
    return jax.shard_map(
        per_device, mesh=mesh, in_specs=(spec, spec), out_specs=(spec, spec), check_vma=False
    )
```

```python
import math
import jax
import jax.numpy as jnp
from jax import lax
from jax.experimental import pallas as pl
from jax.experimental.pallas import tpu as pltpu
from jax.sharding import PartitionSpec as P

RECOVERY_STEPS = 4
PAIRS = ((0, 0), (0, 1), (0, 2), (1, 1), (1, 2), (2, 2))
FOUR_PI = 4.0 * math.pi
PACK = 93
Z_TILE = 2
PADX, PADY = 10, 12
PLACE = (
    [(1, s) for s in range(8)]
    + [(2, 0), (2, 1), (2, 2)]
    + [(3, s) for s in range(7)]
    + [(2, 3), (2, 4), (2, 5), (3, 7)]
)


def slot(i, j):
    return PAIRS.index((min(i, j), max(i, j)))


def aligned(start):
    return pl.ds(start if isinstance(start, int) else pl.multiple_of(start, 8), 8)


def row_of(t, xp, yp):
    return ((t * PADX + xp) * PADY + yp) * 8


def lanes():
    return lax.broadcasted_iota(jnp.int32, (8, 128), 1)


def rows_iota():
    return lax.broadcasted_iota(jnp.int32, (8, 128), 0)


def lroll(v, amount):
    amount = amount % 128
    return v if amount == 0 else pltpu.roll(v, amount, 1)


def shifted(f, halo, k, lane):
    if k > 0:
        return lroll(jnp.where(lane < k, halo, f), 128 - k)
    return lroll(jnp.where(lane >= 128 + k, halo, f), -k)


def d_one(m2, m1, p1, p2):
    return (8.0 / 12.0) * (p1 - m1) - (1.0 / 12.0) * (p2 - m2)


def line_derivs(v, second):
    s1 = v[1] + v[-1]
    s2 = v[2] + v[-2]
    s3 = v[3] + v[-3]
    first = (8.0 / 12.0) * (v[1] - v[-1]) - (1.0 / 12.0) * (v[2] - v[-2])
    kreiss = (0.2 / 64.0) * s3 - (0.2 * 6.0 / 64.0) * s2 + (0.2 * 15.0 / 64.0) * s1
    sec = None
    if second:
        sec = (16.0 / 12.0) * s1 - (1.0 / 12.0) * s2 - (30.0 / 12.0) * v[0]
    return first, kreiss, sec


def fanned(v, amount):
    if amount + 21 >= 128:
        v, amount = lroll(v, amount), 0
    return pltpu.roll(v, amount, 1, stride=3, stride_axis=0)


def expand(lo, hi, t, lane):
    up = fanned(hi, 128 - PACK + 24 * t)
    dn = fanned(lo, 125 - PACK + 24 * t)
    return jnp.where(lane < 3, up, dn)


def tile_at(T, t, xp, yp):
    return T[aligned(row_of(t, xp, yp)), :]


def packed_at(T, xp, yp):
    base = row_of(Z_TILE, xp, yp)
    return [jnp.broadcast_to(T[pl.ds(base + 6 + side, 1), :], (8, 128)) for side in range(2)]


def deriv_at(q, t, xy):
    return aligned(((q * 3 + t - 1) * 16 + xy) * 8)


NEAR = (-2, -1, 1, 2)


def by_four(column):
    def body(x, carry):
        for y in range(4):
            column(4 * x + y)
        return carry

    lax.fori_loop(0, 4, body, 0)


def deriv_xz(T, G, tiles):
    lane = lanes()

    def column(xy):
        xp, yp = xy // 4 + 3, xy % 4 + 4
        own = packed_at(T, xp, yp)
        around = [packed_at(T, xp + a, yp) for a in NEAR]
        border = [d_one(*[around[i][side] for i in range(4)]) for side in range(2)]
        for t in tiles:
            second = t < 3
            vx = {a: tile_at(T, t, xp + a, yp) for a in range(-3, 4)}
            halo = expand(own[0], own[1], t, lane)
            vz = {a: shifted(vx[0], halo, a, lane) if a else vx[0] for a in range(-3, 4)}
            dx, kx, sx = line_derivs(vx, second)
            dz, kz, sz = line_derivs(vz, second)
            G[deriv_at(0, t, xy), :] = dx
            G[deriv_at(2, t, xy), :] = dz
            G[deriv_at(3, t, xy), :] = kx + kz - (0.2 * 60.0 / 64.0) * vx[0]
            if second:
                cross = expand(border[0], border[1], t, lane)
                G[deriv_at(4, t, xy), :] = sx
                G[deriv_at(6, t, xy), :] = d_one(*[shifted(dx, cross, a, lane) for a in NEAR])
                G[deriv_at(9, t, xy), :] = sz

    by_four(column)


def deriv_y(T, G, tiles):
    lane = lanes()

    def column(xy):
        xp, yp = xy // 4 + 3, xy % 4 + 4
        around = [packed_at(T, xp, yp + a) for a in NEAR]
        border = [d_one(*[around[i][side] for i in range(4)]) for side in range(2)]
        for t in tiles:
            second = t < 3
            vy = {a: tile_at(T, t, xp, yp + a) for a in range(-3, 4)}
            dy, ky, sy = line_derivs(vy, second)
            G[deriv_at(1, t, xy), :] = dy
            G[deriv_at(3, t, xy), :] = G[deriv_at(3, t, xy), :] + ky
            if second:
                cross = expand(border[0], border[1], t, lane)
                G[deriv_at(7, t, xy), :] = sy
                G[deriv_at(8, t, xy), :] = d_one(*[shifted(dy, cross, a, lane) for a in NEAR])

    by_four(column)


def deriv_xy(T, G, tiles):
    def column(xy):
        xp, yp = xy // 4 + 3, xy % 4 + 4
        for t in tiles:
            rows = [d_one(*[tile_at(T, t, xp + a, yp + b) for b in NEAR]) for a in NEAR]
            G[deriv_at(5, t, xy), :] = d_one(*rows)

    by_four(column)


def dot3(a, b):
    return a[0] * b[0] + a[1] * b[1] + a[2] * b[2]


def recover(cons, mag):
    density = cons[0]
    mom = cons[1:4]
    energy = cons[4] + density
    mom_sq = dot3(mom, mom)
    mag_sq = dot3(mag, mag)
    cross = dot3(mom, mag)
    cross_sq = cross * cross

    def state(z):
        zb = z + mag_sq
        zz = z * z
        speed_sq = (mom_sq * zz + cross_sq * (2.0 * z + mag_sq)) / (zz * zb * zb)
        ilsq = 1.0 - jnp.minimum(speed_sq, 0.99)
        rho = density * jnp.sqrt(ilsq)
        return ilsq, rho, 0.5 * (z * ilsq - rho)

    z = jnp.maximum(energy - 0.5 * mag_sq, density)
    for _ in range(RECOVERY_STEPS):
        ilsq, rho, p = state(z)
        res = z + mag_sq - p - 0.5 * mag_sq * ilsq - 0.5 * cross_sq / (z * z) - energy
        z = jnp.maximum(z - res / (1.0 - 0.5 * ilsq), density)
    ilsq, rho, p = state(z)
    p = jnp.maximum(p, 0.01 * rho)
    lor = 1.0 / jnp.sqrt(ilsq)
    factor = lor / (z + mag_sq)
    cz = cross / z
    return rho, p, [factor * (mom[i] + cz * mag[i]) for i in range(3)]


def prim_stage(T, PR, PH, EC, EH, columns, halo_columns):
    lane = lanes()

    def strip(t, s, xp, dy=0):
        return T[pl.ds(row_of(t, xp + 1, 2 + dy) + s, 8, stride=8), :]

    def finish(cons, low, up, chi, lapse):
        root = chi * jnp.sqrt(chi)
        centred = [0.5 * (low[i] + up[i]) for i in range(3)]
        mag = [c * root for c in centred]
        rho, p, u = recover([c * root for c in cons], mag)
        inv = -lapse / jnp.sqrt(1.0 + dot3(u, u))
        vel = [a * inv for a in u]
        ele = [
            vel[(i + 1) % 3] * centred[(i + 2) % 3] - vel[(i + 2) % 3] * centred[(i + 1) % 3]
            for i in range(3)
        ]
        return [rho, p] + u + mag, ele

    def body(xp):
        own = [strip(0, s, xp) for s in range(8)]
        zhi = strip(Z_TILE, 7, xp)
        upper = [
            strip(0, 5, xp + 1),
            strip(0, 6, xp, 1),
            jnp.where(lane == 127, lroll(zhi, 127 - (PACK - 21)), lroll(own[7], 127)),
        ]
        prims, ele = finish(own[:5], own[5:], upper, strip(1, 0, xp), strip(1, 7, xp))
        at = aligned(8 + xp * 8)
        for q in range(8):
            PR[q, at, :] = prims[q]
        for i in range(3):
            EC[i, at, :] = ele[i]

    for xp in columns:
        body(xp)

    def body_h(k):
        xp = k + 1

        def halo(u, xq, dy=0):
            p = PACK - 3 * u
            return jnp.where(
                lane < 3, lroll(strip(Z_TILE, 7, xq, dy), -p), lroll(strip(Z_TILE, 6, xq, dy), 125 - p)
            )

        vals = [halo(u, xp) for u in range(9)]
        inner = T[pl.ds(row_of(0, xp + 1, 2) + 7, 8, stride=8), :]
        upper = [
            halo(5, xp + 1),
            halo(6, xp, 1),
            lroll(jnp.where(lane == 0, inner, vals[7]), 127),
        ]
        prims, ele = finish(vals[:5], vals[5:8], upper, vals[8], halo(15, xp))
        at = aligned(8 + k * 8)
        for q in range(8):
            PH[q, at, :] = prims[q]
        for i in range(3):
            EH[i, at, :] = ele[i]

    for k in halo_columns:
        body_h(k)


def limited(a, b):
    return jnp.maximum(jnp.minimum(a, b), 0.0) + jnp.minimum(jnp.maximum(a, b), 0.0)


def stress_parts(rho, p, u, mag):
    lor_sq = 1.0 + dot3(u, u)
    lor = jnp.sqrt(lor_sq)
    inv = 1.0 / lor
    vel = [a * inv for a in u]
    along = dot3(vel, mag)
    b0 = lor * along
    b = [mag[i] * inv + b0 * vel[i] for i in range(3)]
    bsq = dot3(mag, mag) * (inv * inv) + along * along
    enth = rho + 2.0 * p
    inertia = enth + bsq
    return lor, lor_sq, vel, b0, b, bsq, enth, inertia, p + 0.5 * bsq


def face_state(rho, p, u, mag, d):
    lor, lor_sq, vel, b0, b, bsq, enth, inertia, ptot = stress_parts(rho, p, u, mag)
    dens = rho * lor
    wl = inertia * lor_sq
    mom = [wl * vel[j] - b0 * b[j] for j in range(3)]
    cons = [dens] + mom + [wl - ptot - b0 * b0 - dens]
    wv = wl * vel[d]
    flux = [dens * vel[d]]
    for j in range(3):
        f = wv * vel[j] - b[d] * b[j]
        flux.append(f + ptot if j == d else f)
    flux.append(mom[d] - dens * vel[d])
    vsq = dot3(vel, vel)
    cs = 2.0 * p / enth
    va = bsq / inertia
    a2 = cs + va - cs * va
    vd = vel[d]
    spread = jnp.sqrt(a2 * (1.0 - vsq) * (1.0 - vsq * a2 - vd * vd * (1.0 - a2)))
    mid = vd * (1.0 - a2)
    fast = jnp.maximum(jnp.abs(mid + spread), jnp.abs(mid - spread)) / (1.0 - vsq * a2)
    return cons, flux, fast


def face_flux(left, right, normal, chi, lapse, d):
    root = chi * jnp.sqrt(chi)
    states = []
    for side in (left, right):
        mag = list(side[5:8])
        mag[d] = normal * root
        states.append(face_state(side[0], side[1], side[2:5], mag, d))
    (cl, fl, sl), (cr, fr, sr) = states
    sig = jnp.maximum(sl, sr)
    weight = 0.5 * lapse / root
    return [weight * (fl[q] + fr[q] - sig * (cr[q] - cl[q])) for q in range(5)]


def recon(m2, m1, c0, p1):
    mid = c0 - m1
    return m1 + 0.5 * limited(m1 - m2, mid), c0 - 0.5 * limited(mid, p1 - c0)


def flux_stage(T, PR, PH, FX, HR):
    lane = lanes()

    def strip(t, s, x, dy=0):
        return T[pl.ds(row_of(t, x + 3, 2 + dy) + s, 8, stride=8), :]

    def prim(q, x, dy=0):
        return PR[q, pl.ds(8 + (x + 2) * 8 + dy, 8), :]

    def half(a, b):
        return 0.5 * (a + b)

    def body_x(i):
        both = [recon(*[prim(q, i + a) for a in (-2, -1, 0, 1)]) for q in range(8)]
        chi = half(strip(1, 0, i - 1), strip(1, 0, i))
        lapse = half(strip(1, 7, i - 1), strip(1, 7, i))
        out = face_flux([b[0] for b in both], [b[1] for b in both], strip(0, 5, i), chi, lapse, 0)
        at = aligned(i * 8)
        for q in range(5):
            FX[q, at, :] = out[q]

    for i in range(5):
        body_x(i)

    def body(x):
        at = aligned(x * 8)
        up = aligned(x * 8 + 8)
        chi0, lapse0 = strip(1, 0, x), strip(1, 7, x)
        both = [recon(*[prim(q, x, a) for a in (-2, -1, 0, 1)]) for q in range(8)]
        chi = half(strip(1, 0, x, -1), chi0)
        lapse = half(strip(1, 7, x, -1), lapse0)
        fy = face_flux([b[0] for b in both], [b[1] for b in both], strip(0, 6, x), chi, lapse, 1)
        zlo, zhi = strip(Z_TILE, 6, x), strip(Z_TILE, 7, x)

        def halo(u):
            p = PACK - 3 * u
            return jnp.where(lane < 3, lroll(zhi, -p), lroll(zlo, 125 - p))

        chih, lapseh = halo(8), halo(15)
        own = [prim(q, x) for q in range(8)]
        hal = [PH[q, aligned(8 + (x + 1) * 8), :] for q in range(8)]
        both = [
            recon(
                shifted(own[q], hal[q], -2, lane),
                shifted(own[q], hal[q], -1, lane),
                own[q],
                shifted(own[q], hal[q], 1, lane),
            )
            for q in range(8)
        ]
        bz = strip(0, 7, x)
        fz = face_flux(
            [b[0] for b in both],
            [b[1] for b in both],
            bz,
            half(shifted(chi0, chih, -1, lane), chi0),
            half(shifted(lapse0, lapseh, -1, lane), lapse0),
            2,
        )
        both = [
            recon(lroll(own[q], 2), lroll(own[q], 1), hal[q], lroll(hal[q], 127)) for q in range(8)
        ]
        fl = face_flux(
            [b[0] for b in both],
            [b[1] for b in both],
            halo(7),
            half(lroll(chi0, 1), chih),
            half(lroll(lapse0, 1), lapseh),
            2,
        )
        for q in range(5):
            FX[5 + q, at, :] = fy[q]
        for q in range(5):
            fzu = lroll(jnp.where(lane == 0, fl[q], fz[q]), 127)
            fyu = FX[5 + q, pl.ds(x * 8 + 1, 8), :]
            HR[q, at, :] = (fz[q] - fzu) + (fy[q] - fyu) + (FX[q, at, :] - FX[q, up, :])

    for x in range(4):
        body(x)


def field_stage(EC, EH, EZ, HR):
    lane = lanes()

    def ec(i, x, dy=0):
        return EC[i, pl.ds(8 + (x + 2) * 8 + dy, 8), :]

    def eh(i, x, dy=0):
        return EH[i, pl.ds(8 + (x + 1) * 8 + dy, 8), :]

    for x in range(5):
        at = pl.ds(x * 8, 8)
        EZ[0, at, :] = 0.25 * (ec(2, x - 1, -1) + ec(2, x, -1) + ec(2, x - 1) + ec(2, x))
        s = ec(1, x - 1) + ec(1, x)
        h = eh(1, x - 1) + eh(1, x)
        EZ[1, at, :] = 0.25 * (shifted(s, h, -1, lane) + s)
        EZ[2, at, :] = 0.25 * (shifted(s, h, 1, lane) + s)
        if x < 4:
            s = ec(0, x, -1) + ec(0, x)
            h = eh(0, x, -1) + eh(0, x)
            EZ[3, at, :] = 0.25 * (shifted(s, h, -1, lane) + s)
            EZ[4, at, :] = 0.25 * (shifted(s, h, 1, lane) + s)
    for x in range(4):
        at, up, yu = pl.ds(x * 8, 8), pl.ds(x * 8 + 8, 8), pl.ds(x * 8 + 1, 8)
        ez = EZ[0, at, :]
        HR[5, at, :] = (EZ[2, at, :] - EZ[1, at, :]) - (EZ[0, yu, :] - ez)
        HR[6, at, :] = (EZ[0, up, :] - ez) - (EZ[4, at, :] - EZ[3, at, :])
        HR[7, at, :] = (EZ[3, yu, :] - EZ[3, at, :]) - (EZ[1, up, :] - EZ[1, at, :])


def sym(values):
    return [[values[slot(i, j)] for j in range(3)] for i in range(3)]


def trace(inv, m):
    return (
        inv[0][0] * m[0][0]
        + inv[1][1] * m[1][1]
        + inv[2][2] * m[2][2]
        + 2.0 * (inv[0][1] * m[0][1] + inv[0][2] * m[0][2] + inv[1][2] * m[1][2])
    )


def inverse(g):
    c00 = g[1][1] * g[2][2] - g[1][2] * g[1][2]
    c01 = g[0][2] * g[1][2] - g[0][1] * g[2][2]
    c02 = g[0][1] * g[1][2] - g[0][2] * g[1][1]
    c11 = g[0][0] * g[2][2] - g[0][2] * g[0][2]
    c12 = g[0][1] * g[0][2] - g[0][0] * g[1][2]
    c22 = g[0][0] * g[1][1] - g[0][1] * g[0][1]
    r = 1.0 / (g[0][0] * c00 + g[0][1] * c01 + g[0][2] * c02)
    return sym([c00 * r, c01 * r, c02 * r, c11 * r, c12 * r, c22 * r])


R3 = range(3)


def algebra_stage(G, PR, HR, o_st, o_fl, RT):
    low = rows_iota() < 4

    def body(h, carry):
        x = 2 * h

        def fold(a, b):
            return jnp.where(low, a, b)

        at = aligned(8 * h)

        def strip(ref, q, pad):
            return fold(
                ref[q, pl.ds(pad + x * 8 + 2, 8), :], ref[q, pl.ds(pad + x * 8 + 8 - 2, 8), :]
            )

        def g(q, v):
            t, s = PLACE[v]
            return G[pl.ds(((q * 3 + t - 1) * 16 + 8 * h) * 8 + s, 8, stride=8), :]

        cur = [o_st[v, at, :] for v in range(22)]
        flu = [o_fl[v, at, :] for v in range(8)]
        prims = [strip(PR, q, 8 + 16) for q in range(8)]

        def grad(v):
            return [g(k, v) for k in R3]

        def hess(v):
            return sym([g(4 + s, v) for s in range(6)])

        chi, lapse = cur[0], cur[7]
        metric = sym(cur[1:7])
        shift = cur[8:11]
        khat, theta = cur[11], cur[21]
        trl = sym(cur[12:18])
        conn = cur[18:21]
        inv = inverse(metric)
        ichi = 1.0 / chi
        root = chi * jnp.sqrt(chi)
        ktot = khat + 2.0 * theta

        lor, lor_sq, vel, b0, b, bsq, enth, inertia, ptot = stress_parts(
            prims[0], prims[1], prims[2:5], prims[5:8]
        )
        wl = inertia * lor_sq
        stress = sym(
            [
                wl * vel[i] * vel[j] - b[i] * b[j] + (ptot if i == j else 0.0)
                for i, j in PAIRS
            ]
        )
        total = flu[4] + flu[0]
        dens = total * root
        mom = [flu[1 + i] * root for i in R3]
        dal = grad(7)
        dsh = [grad(8 + i) for i in R3]
        hydro = [strip(HR, q, 0) for q in range(8)]
        for i in R3:
            hydro[1 + i] = (
                hydro[1 + i]
                - total * dal[i]
                + (flu[1] * dsh[0][i] + flu[2] * dsh[1][i] + flu[3] * dsh[2][i])
            )
        third = ktot * (1.0 / 3.0)
        curv = sym([(trl[i][j] + metric[i][j] * third) * ichi for i, j in PAIRS])
        tk = (
            stress[0][0] * curv[0][0]
            + stress[1][1] * curv[1][1]
            + stress[2][2] * curv[2][2]
            + 2.0
            * (stress[0][1] * curv[0][1] + stress[0][2] * curv[0][2] + stress[1][2] * curv[1][2])
        )
        hydro[4] = hydro[4] + lapse / root * tk - dot3(flu[1:4], dal)
        for q in range(8):
            RT[22 + q, at, :] = hydro[q]

        def adv(gr):
            return shift[0] * gr[0] + shift[1] * gr[1] + shift[2] * gr[2]

        def emit(v, rate):
            RT[v, at, :] = rate + g(3, v)

        dg = [[grad(1 + slot(i, j)) if i <= j else None for j in R3] for i in R3]
        dg = [[dg[min(i, j)][max(i, j)] for j in R3] for i in R3]
        lowered = [
            sym([0.5 * (dg[i][k][j] + dg[i][j][k] - dg[j][k][i]) for j, k in PAIRS]) for i in R3
        ]
        raised = [
            sym(
                [
                    inv[i][0] * lowered[0][j][k]
                    + inv[i][1] * lowered[1][j][k]
                    + inv[i][2] * lowered[2][j][k]
                    for j, k in PAIRS
                ]
            )
            for i in R3
        ]
        gd = [trace(inv, raised[i]) for i in R3]
        dchi = grad(0)
        hchi = hess(0)
        xcov = sym(
            [hchi[i][j] - dot3([raised[k][i][j] for k in R3], dchi) for i, j in PAIRS]
        )
        chi_lap = trace(inv, xcov)
        uchi = [dot3(inv[i], dchi) for i in R3]
        chi_sq = dot3(uchi, dchi)
        cross = dot3(uchi, dal)
        hal = hess(7)
        half_ichi = 0.5 * ichi
        lcov = sym(
            [
                hal[i][j]
                - dot3([raised[k][i][j] for k in R3], dal)
                + (dchi[i] * dal[j] + dchi[j] * dal[i] - metric[i][j] * cross) * half_ichi
                for i, j in PAIRS
            ]
        )
        lapse_lap = chi * trace(inv, lcov)
        dgam = [grad(18 + i) for i in R3]
        cu = [
            [
                [
                    inv[l][0] * lowered[j][k][0]
                    + inv[l][1] * lowered[j][k][1]
                    + inv[l][2] * lowered[j][k][2]
                    for l in R3
                ]
                for k in R3
            ]
            for j in R3
        ]
        quarter = half_ichi * half_ichi
        ricci = []
        for i, j in PAIRS:
            v = 1 + slot(i, j)
            hg = hess(v)
            r = -0.5 * trace(inv, hg)
            for k in R3:
                r = r + 0.5 * (metric[k][i] * dgam[k][j] + metric[k][j] * dgam[k][i])
                r = r + 0.5 * gd[k] * (lowered[i][j][k] + lowered[j][i][k])
            for k in R3:
                for l in R3:
                    r = r + raised[k][l][i] * cu[j][k][l]
                    r = r + raised[k][l][j] * cu[i][k][l]
                    r = r + raised[k][i][l] * cu[k][j][l]
            r = r + (xcov[i][j] + metric[i][j] * chi_lap) * half_ichi
            r = r - (dchi[i] * dchi[j] + 3.0 * metric[i][j] * chi_sq) * quarter
            ricci.append(r)
        ricci = sym(ricci)
        rscal = chi * trace(inv, ricci)
        strace = chi * trace(inv, stress)
        mixed = [[dot3(inv[i], [trl[k][j] for k in R3]) for j in R3] for i in R3]
        up = sym([dot3(mixed[i], inv[j]) for i, j in PAIRS])
        aa = trace(trl, up)
        div = dsh[0][0] + dsh[1][1] + dsh[2][2]
        div23 = (2.0 / 3.0) * div

        emit(0, adv(dchi) + (2.0 / 3.0) * chi * (lapse * ktot - div))
        emit(7, adv(dal) - 2.0 * lapse * khat)
        for i in R3:
            emit(8 + i, adv(dsh[i]) + 0.75 * conn[i] - shift[i])
        dkh = grad(11)
        dth = grad(21)
        emit(
            11,
            adv(dkh)
            - lapse_lap
            + lapse * (aa + ktot * third)
            + FOUR_PI * lapse * (strace + dens)
            + 0.02 * lapse * theta,
        )
        src = sym(
            [
                -lcov[i][j] + lapse * (ricci[i][j] - (2.0 * FOUR_PI) * stress[i][j])
                for i, j in PAIRS
            ]
        )
        strc = trace(inv, src) * (1.0 / 3.0)
        for i, j in PAIRS:
            s = slot(i, j)
            acc = adv(dg[i][j])
            for k in R3:
                acc = acc + metric[i][k] * dsh[k][j] + metric[j][k] * dsh[k][i]
            emit(1 + s, acc - metric[i][j] * div23 - 2.0 * lapse * trl[i][j])
            prod = dot3(trl[i], [mixed[k][j] for k in R3])
            acc = adv(grad(12 + s))
            for k in R3:
                acc = acc + trl[i][k] * dsh[k][j] + trl[j][k] * dsh[k][i]
            emit(
                12 + s,
                acc
                - trl[i][j] * div23
                + chi * (src[i][j] - metric[i][j] * strc)
                + lapse * (ktot * trl[i][j] - 2.0 * prod),
            )
        hsh = [hess(8 + i) for i in R3]
        ddiv = [hsh[0][0][j] + hsh[1][1][j] + hsh[2][2][j] for j in R3]
        for i in R3:
            br = trace(up, raised[i])
            br = br - 1.5 * ichi * dot3(up[i], dchi)
            br = br - (1.0 / 3.0) * dot3(inv[i], [2.0 * dkh[j] + dth[j] for j in R3])
            br = br - (2.0 * FOUR_PI) * dot3(inv[i], mom)
            emit(
                18 + i,
                adv(dgam[i])
                - dot3(gd, dsh[i])
                + gd[i] * div23
                + trace(inv, hsh[i])
                + (1.0 / 3.0) * dot3(inv[i], ddiv)
                - 2.0 * dot3(up[i], dal)
                + 2.0 * lapse * br
                - 0.04 * lapse * (conn[i] - gd[i]),
            )
        emit(
            21,
            adv(dth)
            + 0.5
            * lapse
            * (rscal - aa + (2.0 / 3.0) * ktot * ktot - (4.0 * FOUR_PI) * dens)
            - 0.04 * lapse * theta,
        )
        return carry

    lax.fori_loop(0, 2, body, 0)


def compute_scratch():
    V = lambda *s: pltpu.VMEM(s, jnp.float32)
    return [
        V(10 * 3 * 16 * 8, 128),
        V(8, 80, 128),
        V(8, 64, 128),
        V(3, 80, 128),
        V(3, 64, 128),
        V(10, 48, 128),
        V(8, 48, 128),
        V(5, 48, 128),
    ]


MESH = pl.DeviceIdType.MESH
PHASES = ((0, 1), (1, 7), (8, 7), (15, 7))
N_SLOTS = 22
N_GREETED = 18


def wave_stage(own):
    metric = sym([own(8 + v) for v in range(1, 7)])
    inv = inverse(metric)
    scale = 2.0 * own(8 + 7) * own(8)
    speeds = [jnp.abs(own(16 + d)) + jnp.sqrt(scale * inv[d][d]) for d in range(3)]
    return jnp.maximum(jnp.maximum(speeds[0], speeds[1]), speeds[2])


def load_stage(st, fl, o_st, o_fl, T, tiles):
    for u in range(30):
        src, dst, v = (fl, o_fl, u) if u < 8 else (st, o_st, u - 8)
        t, s = (0, u) if u < 8 else PLACE[v]
        if t not in tiles:
            continue
        for x in range(4):
            value = src[v, x]
            T[pl.ds(row_of(t, x + 3, 4) + s, 4, stride=8), :] = value
            dst[v, pl.ds(4 * x, 4), :] = value


def speed_stage(st, mine):
    top = None
    for x in range(4):

        def own(u):
            return st[u - 8, x]

        speed = wave_stage(own)
        top = speed if top is None else jnp.maximum(top, speed)
    mine[0] = jnp.max(top, axis=0, keepdims=True)


def border_stage(o_st, o_fl, zsend):
    lane = lanes()

    def body(h, carry):
        at = pl.ds(pl.multiple_of(8 * h, 8), 8)
        last = jnp.zeros((8, 128), jnp.float32)
        first = jnp.zeros((8, 128), jnp.float32)
        for u in range(30):
            t, s = (0, u) if u < 8 else PLACE[u - 8]
            p = PACK - 3 * (8 * t + s)
            here = (lane >= p) & (lane < p + 3)
            value = o_fl[u, at, :] if u < 8 else o_st[u - 8, at, :]
            first = jnp.where(here, lroll(value, p), first)
            last = jnp.where(here, lroll(value, p - 125), last)
        zsend[0, at, :] = last
        zsend[1, at, :] = first
        return carry

    lax.fori_loop(0, 2, body, 0)


def halo_rows(zrecv, T):
    for side in range(2):
        for x in range(4):
            T[pl.ds(row_of(Z_TILE, x + 3, 4) + 6 + side, 4, stride=8), :] = zrecv[
                side, pl.ds(4 * x, 4), :
            ]


def kernel(st_in, fl_in, o_st, o_fl, st, fl, insem, T5, zsend, zrecv, mine, slots, RT, ssem, rsem, msem, known, *scratch):
    gx, gy, gz = lax.axis_index("gx"), lax.axis_index("gy"), lax.axis_index("gz")
    hi, core = gy & 1, gx & 1
    T = T5.reshape(3840, 128)

    def at_x(step):
        x2 = (hi * 4 + gz + step) & 7
        return (gx, gy - hi + (x2 >> 2), x2 & 3)

    mate = (gx + 1 - 2 * core, gy, gz)
    ring_x = [at_x(k) for k in range(1, 8)]
    ring_y = [(gx, (gy + 2 * k) & 15, gz) for k in range(1, 8)]
    ring_z = [((gx + 2 * k) & 15, gy, gz) for k in range(1, 8)]
    x_up, x_dn = ((gx + 1) & 15, gy, gz), ((gx + 15) & 15, gy, gz)
    z_up, z_dn = (gx, gy, (gz + 1) & 3), (gx, gy, (gz + 3) & 3)
    y_up, y_dn = ring_y[0], ring_y[6]
    cross = ((gx + 15 + 2 * core) & 15, gy, gz)
    partner = ring_x[3]
    onward = (gx, (gy + 2 - 4 * hi) & 15, gz)

    barrier = pltpu.get_barrier_semaphore()
    for peer in [partner, mate, cross, y_up, y_dn] + ring_x[:3] + ring_x[4:] + ring_z:
        pl.semaphore_signal(barrier, inc=1, device_id=peer, device_id_type=MESH)
    fetched = [
        pltpu.make_async_copy(st_in, st, insem.at[0]),
        pltpu.make_async_copy(fl_in, fl, insem.at[1]),
    ]
    for copy in fetched:
        copy.start()
    fetched[0].wait()
    speed_stage(st, mine)
    load_stage(st, fl, o_st, o_fl, T, (1,))
    fetched[1].wait()
    load_stage(st, fl, o_st, o_fl, T, (0,))
    load_stage(st, fl, o_st, o_fl, T, (2, 3))
    border_stage(o_st, o_fl, zsend)
    pl.semaphore_wait(barrier, N_GREETED)

    def tell(step):
        for peer in (y_up, y_dn):
            pl.semaphore_signal(known.at[step], inc=1, device_id=peer, device_id_type=MESH)

    def told(step):
        pl.semaphore_wait(known.at[step], 2)

    started = []

    def send(src, dst, peer):
        k = len(started)
        copy = pltpu.make_async_remote_copy(
            src_ref=src,
            dst_ref=dst,
            send_sem=ssem.at[k],
            recv_sem=rsem.at[k],
            device_id=peer,
            device_id_type=MESH,
        )
        copy.start()
        started.append(copy)
        return copy

    def share(phase, peers):
        base = PHASES[phase][0]
        for k, peer in enumerate(peers):
            pltpu.make_async_remote_copy(
                src_ref=mine.at[phase],
                dst_ref=slots.at[base + k],
                send_sem=msem.at[phase],
                recv_sem=msem.at[4 + phase],
                device_id=peer,
                device_id_type=MESH,
            ).start()

    def gathered(phase):
        part = slots.at[pl.ds(*PHASES[phase])]
        pltpu.make_async_copy(part, part, msem.at[4 + phase]).wait()
        mine[phase + 1] = jnp.maximum(mine[phase], jnp.max(slots[pl.ds(*PHASES[phase])], axis=0))

    def drained(phase):
        part = slots.at[pl.ds(*PHASES[phase])]
        pltpu.make_async_copy(part, part, msem.at[phase]).wait()

    def block(t, n, xp, nx, yp, ny):
        return T5.at[pl.ds(t, n), pl.ds(xp, nx), pl.ds(yp, ny)]

    def to_partner(t):
        return send(block(t, 1, 3, 4, 4, 4), block(t, 1, 3, 4, 8 * hi, 4), partner)

    def go_on(t):
        return send(block(t, 1, 3, 4, 9 - 9 * hi, 3), block(t, 1, 3, 4, 1 + 7 * hi, 3), onward)

    def faces(t, n):
        return [
            send(block(t, n, 3, 3, 4, 4), block(t, n, 7, 3, 4, 4), x_dn),
            send(block(t, n, 4, 3, 4, 4), block(t, n, 0, 3, 4, 4), x_up),
        ]

    def edges(t, n):
        copies = []
        for yp in (2, 8):
            copies.append(send(block(t, n, 3, 2, yp, 2), block(t, n, 7, 2, yp, 2), x_dn))
            copies.append(send(block(t, n, 5, 2, yp, 2), block(t, n, 1, 2, yp, 2), x_up))
        return copies

    G, PR, PH, EC, EH, FX, HR, EZ = scratch
    far, relay, side = {}, {}, {}
    share(0, [mate])
    tell(0)
    zs = [send(zsend.at[0], zrecv.at[0], z_up), send(zsend.at[1], zrecv.at[1], z_dn)]
    for t in range(2):
        far[t] = to_partner(t)
    front = faces(0, 2)
    for copy in zs:
        copy.wait_recv()
    halo_rows(zrecv, T)
    for t in (2, 3):
        far[t] = to_partner(t)
    gathered(0)
    share(1, ring_z)
    front += faces(2, 2)
    told(0)
    tell(1)
    for copy in front:
        copy.wait_recv()
    deriv_xz(T, G, (1,))
    far[0].wait_recv()
    relay[0] = go_on(0)
    gathered(1)
    share(2, ring_x)
    told(1)
    tell(2)
    deriv_xz(T, G, (2,))
    far[1].wait_recv()
    relay[1] = go_on(1)
    far[2].wait_recv()
    relay[2] = go_on(2)
    for t in range(2):
        relay[t].wait_recv()
        side[t] = edges(t, 1)
    gathered(2)
    told(2)
    share(3, ring_y)
    far[3].wait_recv()
    relay[3] = go_on(3)
    relay[2].wait_recv()
    side[2] = edges(2, 1)
    deriv_xz(T, G, (3,))
    prim_stage(T, PR, PH, EC, EH, (2, 3, 4), (1, 2, 3))
    deriv_y(T, G, (1, 2))
    relay[3].wait_recv()
    deriv_y(T, G, (3,))
    for t in range(3):
        for copy in side[t]:
            copy.wait_recv()
    deriv_xy(T, G, (1, 2))
    prim_stage(T, PR, PH, EC, EH, (0, 1, 5, 6, 7), (0, 4, 5))
    flux_stage(T, PR, PH, FX, HR)
    field_stage(EC, EH, EZ, HR)
    algebra_stage(G, PR, HR, o_st, o_fl, RT)
    gathered(3)
    step = 0.25 / jnp.max(mine[4], axis=1, keepdims=True)
    for v in range(22):
        o_st[v] = o_st[v] + step * RT[v]
    for v in range(8):
        o_fl[v] = o_fl[v] + step * RT[22 + v]
    for copy in started:
        copy.wait_send()
    for phase in range(4):
        drained(phase)


def per_device(spacetime, fluid):
    vmem = pl.BlockSpec(memory_space=pltpu.VMEM)
    space = lambda *s: pltpu.VMEM(s, jnp.float32)
    st_new, fl_new = pl.pallas_call(
        kernel,
        out_shape=(
            jax.ShapeDtypeStruct((22, 16, 128), jnp.float32),
            jax.ShapeDtypeStruct((8, 16, 128), jnp.float32),
        ),
        in_specs=[pl.BlockSpec(memory_space=pltpu.HBM)] * 2,
        out_specs=(vmem, vmem),
        scratch_shapes=[
            space(22, 4, 4, 128),
            space(8, 4, 4, 128),
            pltpu.SemaphoreType.DMA((2,)),
            space(4, PADX, PADY, 8, 128),
            space(2, 16, 128),
            space(2, 16, 128),
            space(5, 1, 128),
            space(N_SLOTS, 1, 128),
            space(30, 16, 128),
            pltpu.SemaphoreType.DMA((32,)),
            pltpu.SemaphoreType.DMA((32,)),
            pltpu.SemaphoreType.DMA((8,)),
            pltpu.SemaphoreType.REGULAR((3,)),
        ]
        + compute_scratch(),
        compiler_params=pltpu.CompilerParams(
            collective_id=1, has_side_effects=True, vmem_limit_bytes=56164352
        ),
    )(spacetime, fluid)
    return st_new.reshape(22, 4, 4, 128), fl_new.reshape(8, 4, 4, 128)


def solution(mesh):
    spec = P(None, "gx", "gy", "gz")
    return jax.shard_map(
        per_device, mesh=mesh, in_specs=(spec, spec), out_specs=(spec, spec), check_vma=False
    )
```

```python
import math
import jax
import jax.numpy as jnp
from jax import lax
from jax.experimental import pallas as pl
from jax.experimental.pallas import tpu as pltpu
from jax.sharding import PartitionSpec as P

RECOVERY_STEPS = 4
PAIRS = ((0, 0), (0, 1), (0, 2), (1, 1), (1, 2), (2, 2))
FOUR_PI = 4.0 * math.pi
PACK = 93
Z_TILE = 2
PADX, PADY = 10, 12
PLACE = (
    [(1, s) for s in range(8)]
    + [(2, 0), (2, 1), (2, 2)]
    + [(3, s) for s in range(7)]
    + [(2, 3), (2, 4), (2, 5), (3, 7)]
)


def slot(i, j):
    return PAIRS.index((min(i, j), max(i, j)))


def aligned(start):
    return pl.ds(start if isinstance(start, int) else pl.multiple_of(start, 8), 8)


def row_of(t, xp, yp):
    return ((t * PADX + xp) * PADY + yp) * 8


def lanes():
    return lax.broadcasted_iota(jnp.int32, (8, 128), 1)


def rows_iota():
    return lax.broadcasted_iota(jnp.int32, (8, 128), 0)


def lroll(v, amount):
    amount = amount % 128
    return v if amount == 0 else pltpu.roll(v, amount, 1)


def shifted(f, halo, k, lane):
    if k > 0:
        return lroll(jnp.where(lane < k, halo, f), 128 - k)
    return lroll(jnp.where(lane >= 128 + k, halo, f), -k)


def d_one(m2, m1, p1, p2):
    return (8.0 / 12.0) * (p1 - m1) - (1.0 / 12.0) * (p2 - m2)


def line_derivs(v, second):
    s1 = v[1] + v[-1]
    s2 = v[2] + v[-2]
    s3 = v[3] + v[-3]
    first = (8.0 / 12.0) * (v[1] - v[-1]) - (1.0 / 12.0) * (v[2] - v[-2])
    kreiss = (0.2 / 64.0) * s3 - (0.2 * 6.0 / 64.0) * s2 + (0.2 * 15.0 / 64.0) * s1
    sec = None
    if second:
        sec = (16.0 / 12.0) * s1 - (1.0 / 12.0) * s2 - (30.0 / 12.0) * v[0]
    return first, kreiss, sec


def fanned(v, amount):
    if amount + 21 >= 128:
        v, amount = lroll(v, amount), 0
    return pltpu.roll(v, amount, 1, stride=3, stride_axis=0)


def expand(lo, hi, t, lane):
    up = fanned(hi, 128 - PACK + 24 * t)
    dn = fanned(lo, 125 - PACK + 24 * t)
    return jnp.where(lane < 3, up, dn)


def tile_at(T, t, xp, yp):
    return T[aligned(row_of(t, xp, yp)), :]


def packed_at(T, xp, yp):
    base = row_of(Z_TILE, xp, yp)
    return [jnp.broadcast_to(T[pl.ds(base + 6 + side, 1), :], (8, 128)) for side in range(2)]


def deriv_at(q, t, xy):
    return aligned(((q * 3 + t - 1) * 16 + xy) * 8)


NEAR = (-2, -1, 1, 2)


def by_four(column):
    def body(x, carry):
        for y in range(4):
            column(4 * x + y)
        return carry

    lax.fori_loop(0, 4, body, 0)


def deriv_xz(T, G, tiles):
    lane = lanes()

    def column(xy):
        xp, yp = xy // 4 + 3, xy % 4 + 4
        own = packed_at(T, xp, yp)
        around = [packed_at(T, xp + a, yp) for a in NEAR]
        border = [d_one(*[around[i][side] for i in range(4)]) for side in range(2)]
        for t in tiles:
            second = t < 3
            vx = {a: tile_at(T, t, xp + a, yp) for a in range(-3, 4)}
            halo = expand(own[0], own[1], t, lane)
            vz = {a: shifted(vx[0], halo, a, lane) if a else vx[0] for a in range(-3, 4)}
            dx, kx, sx = line_derivs(vx, second)
            dz, kz, sz = line_derivs(vz, second)
            G[deriv_at(0, t, xy), :] = dx
            G[deriv_at(2, t, xy), :] = dz
            G[deriv_at(3, t, xy), :] = kx + kz - (0.2 * 60.0 / 64.0) * vx[0]
            if second:
                cross = expand(border[0], border[1], t, lane)
                G[deriv_at(4, t, xy), :] = sx
                G[deriv_at(6, t, xy), :] = d_one(*[shifted(dx, cross, a, lane) for a in NEAR])
                G[deriv_at(9, t, xy), :] = sz

    by_four(column)


def deriv_y(T, G, tiles):
    lane = lanes()

    def column(xy):
        xp, yp = xy // 4 + 3, xy % 4 + 4
        around = [packed_at(T, xp, yp + a) for a in NEAR]
        border = [d_one(*[around[i][side] for i in range(4)]) for side in range(2)]
        for t in tiles:
            second = t < 3
            vy = {a: tile_at(T, t, xp, yp + a) for a in range(-3, 4)}
            dy, ky, sy = line_derivs(vy, second)
            G[deriv_at(1, t, xy), :] = dy
            G[deriv_at(3, t, xy), :] = G[deriv_at(3, t, xy), :] + ky
            if second:
                cross = expand(border[0], border[1], t, lane)
                G[deriv_at(7, t, xy), :] = sy
                G[deriv_at(8, t, xy), :] = d_one(*[shifted(dy, cross, a, lane) for a in NEAR])

    by_four(column)


def deriv_xy(T, G, tiles):
    def column(xy):
        xp, yp = xy // 4 + 3, xy % 4 + 4
        for t in tiles:
            rows = [d_one(*[tile_at(T, t, xp + a, yp + b) for b in NEAR]) for a in NEAR]
            G[deriv_at(5, t, xy), :] = d_one(*rows)

    by_four(column)


def dot3(a, b):
    return a[0] * b[0] + a[1] * b[1] + a[2] * b[2]


def recover(cons, mag):
    density = cons[0]
    mom = cons[1:4]
    energy = cons[4] + density
    mom_sq = dot3(mom, mom)
    mag_sq = dot3(mag, mag)
    cross = dot3(mom, mag)
    cross_sq = cross * cross

    def state(z):
        zb = z + mag_sq
        zz = z * z
        speed_sq = (mom_sq * zz + cross_sq * (2.0 * z + mag_sq)) / (zz * zb * zb)
        ilsq = 1.0 - jnp.minimum(speed_sq, 0.99)
        rho = density * jnp.sqrt(ilsq)
        return ilsq, rho, 0.5 * (z * ilsq - rho)

    z = jnp.maximum(energy - 0.5 * mag_sq, density)
    for _ in range(RECOVERY_STEPS):
        ilsq, rho, p = state(z)
        res = z + mag_sq - p - 0.5 * mag_sq * ilsq - 0.5 * cross_sq / (z * z) - energy
        z = jnp.maximum(z - res / (1.0 - 0.5 * ilsq), density)
    ilsq, rho, p = state(z)
    p = jnp.maximum(p, 0.01 * rho)
    lor = 1.0 / jnp.sqrt(ilsq)
    factor = lor / (z + mag_sq)
    cz = cross / z
    return rho, p, [factor * (mom[i] + cz * mag[i]) for i in range(3)]


def prim_stage(T, PR, PH, EC, EH, columns, halo_columns):
    lane = lanes()

    def strip(t, s, xp, dy=0):
        return T[pl.ds(row_of(t, xp + 1, 2 + dy) + s, 8, stride=8), :]

    def finish(cons, low, up, chi, lapse):
        root = chi * jnp.sqrt(chi)
        centred = [0.5 * (low[i] + up[i]) for i in range(3)]
        mag = [c * root for c in centred]
        rho, p, u = recover([c * root for c in cons], mag)
        inv = -lapse / jnp.sqrt(1.0 + dot3(u, u))
        vel = [a * inv for a in u]
        ele = [
            vel[(i + 1) % 3] * centred[(i + 2) % 3] - vel[(i + 2) % 3] * centred[(i + 1) % 3]
            for i in range(3)
        ]
        return [rho, p] + u + mag, ele

    def body(xp):
        own = [strip(0, s, xp) for s in range(8)]
        zhi = strip(Z_TILE, 7, xp)
        upper = [
            strip(0, 5, xp + 1),
            strip(0, 6, xp, 1),
            jnp.where(lane == 127, lroll(zhi, 127 - (PACK - 21)), lroll(own[7], 127)),
        ]
        prims, ele = finish(own[:5], own[5:], upper, strip(1, 0, xp), strip(1, 7, xp))
        at = aligned(8 + xp * 8)
        for q in range(8):
            PR[q, at, :] = prims[q]
        for i in range(3):
            EC[i, at, :] = ele[i]

    for xp in columns:
        body(xp)

    def body_h(k):
        xp = k + 1

        def halo(u, xq, dy=0):
            p = PACK - 3 * u
            return jnp.where(
                lane < 3, lroll(strip(Z_TILE, 7, xq, dy), -p), lroll(strip(Z_TILE, 6, xq, dy), 125 - p)
            )

        vals = [halo(u, xp) for u in range(9)]
        inner = T[pl.ds(row_of(0, xp + 1, 2) + 7, 8, stride=8), :]
        upper = [
            halo(5, xp + 1),
            halo(6, xp, 1),
            lroll(jnp.where(lane == 0, inner, vals[7]), 127),
        ]
        prims, ele = finish(vals[:5], vals[5:8], upper, vals[8], halo(15, xp))
        at = aligned(8 + k * 8)
        for q in range(8):
            PH[q, at, :] = prims[q]
        for i in range(3):
            EH[i, at, :] = ele[i]

    for k in halo_columns:
        body_h(k)


def limited(a, b):
    return jnp.maximum(jnp.minimum(a, b), 0.0) + jnp.minimum(jnp.maximum(a, b), 0.0)


def stress_parts(rho, p, u, mag):
    lor_sq = 1.0 + dot3(u, u)
    lor = jnp.sqrt(lor_sq)
    inv = 1.0 / lor
    vel = [a * inv for a in u]
    along = dot3(vel, mag)
    b0 = lor * along
    b = [mag[i] * inv + b0 * vel[i] for i in range(3)]
    bsq = dot3(mag, mag) * (inv * inv) + along * along
    enth = rho + 2.0 * p
    inertia = enth + bsq
    return lor, lor_sq, vel, b0, b, bsq, enth, inertia, p + 0.5 * bsq


def face_state(rho, p, u, mag, d):
    lor, lor_sq, vel, b0, b, bsq, enth, inertia, ptot = stress_parts(rho, p, u, mag)
    dens = rho * lor
    wl = inertia * lor_sq
    mom = [wl * vel[j] - b0 * b[j] for j in range(3)]
    cons = [dens] + mom + [wl - ptot - b0 * b0 - dens]
    wv = wl * vel[d]
    flux = [dens * vel[d]]
    for j in range(3):
        f = wv * vel[j] - b[d] * b[j]
        flux.append(f + ptot if j == d else f)
    flux.append(mom[d] - dens * vel[d])
    vsq = dot3(vel, vel)
    cs = 2.0 * p / enth
    va = bsq / inertia
    a2 = cs + va - cs * va
    vd = vel[d]
    spread = jnp.sqrt(a2 * (1.0 - vsq) * (1.0 - vsq * a2 - vd * vd * (1.0 - a2)))
    mid = vd * (1.0 - a2)
    fast = jnp.maximum(jnp.abs(mid + spread), jnp.abs(mid - spread)) / (1.0 - vsq * a2)
    return cons, flux, fast


def face_flux(left, right, normal, chi, lapse, d):
    root = chi * jnp.sqrt(chi)
    states = []
    for side in (left, right):
        mag = list(side[5:8])
        mag[d] = normal * root
        states.append(face_state(side[0], side[1], side[2:5], mag, d))
    (cl, fl, sl), (cr, fr, sr) = states
    sig = jnp.maximum(sl, sr)
    weight = 0.5 * lapse / root
    return [weight * (fl[q] + fr[q] - sig * (cr[q] - cl[q])) for q in range(5)]


def recon(m2, m1, c0, p1):
    mid = c0 - m1
    return m1 + 0.5 * limited(m1 - m2, mid), c0 - 0.5 * limited(mid, p1 - c0)


def flux_stage(T, PR, PH, FX, HR, columns, last):
    lane = lanes()

    def strip(t, s, x, dy=0):
        return T[pl.ds(row_of(t, x + 3, 2 + dy) + s, 8, stride=8), :]

    def prim(q, x, dy=0):
        return PR[q, pl.ds(8 + (x + 2) * 8 + dy, 8), :]

    def half(a, b):
        return 0.5 * (a + b)

    def body_x(i):
        both = [recon(*[prim(q, i + a) for a in (-2, -1, 0, 1)]) for q in range(8)]
        chi = half(strip(1, 0, i - 1), strip(1, 0, i))
        lapse = half(strip(1, 7, i - 1), strip(1, 7, i))
        out = face_flux([b[0] for b in both], [b[1] for b in both], strip(0, 5, i), chi, lapse, 0)
        at = aligned(i * 8)
        for q in range(5):
            FX[q, at, :] = out[q]

    for i in range(5 if last else 0):
        body_x(i)

    def body(x):
        at = aligned(x * 8)
        chi0, lapse0 = strip(1, 0, x), strip(1, 7, x)
        both = [recon(*[prim(q, x, a) for a in (-2, -1, 0, 1)]) for q in range(8)]
        chi = half(strip(1, 0, x, -1), chi0)
        lapse = half(strip(1, 7, x, -1), lapse0)
        fy = face_flux([b[0] for b in both], [b[1] for b in both], strip(0, 6, x), chi, lapse, 1)
        zlo, zhi = strip(Z_TILE, 6, x), strip(Z_TILE, 7, x)

        def halo(u):
            p = PACK - 3 * u
            return jnp.where(lane < 3, lroll(zhi, -p), lroll(zlo, 125 - p))

        chih, lapseh = halo(8), halo(15)
        own = [prim(q, x) for q in range(8)]
        hal = [PH[q, aligned(8 + (x + 1) * 8), :] for q in range(8)]
        both = [
            recon(
                shifted(own[q], hal[q], -2, lane),
                shifted(own[q], hal[q], -1, lane),
                own[q],
                shifted(own[q], hal[q], 1, lane),
            )
            for q in range(8)
        ]
        bz = strip(0, 7, x)
        fz = face_flux(
            [b[0] for b in both],
            [b[1] for b in both],
            bz,
            half(shifted(chi0, chih, -1, lane), chi0),
            half(shifted(lapse0, lapseh, -1, lane), lapse0),
            2,
        )
        both = [
            recon(lroll(own[q], 2), lroll(own[q], 1), hal[q], lroll(hal[q], 127)) for q in range(8)
        ]
        fl = face_flux(
            [b[0] for b in both],
            [b[1] for b in both],
            halo(7),
            half(lroll(chi0, 1), chih),
            half(lroll(lapse0, 1), lapseh),
            2,
        )
        for q in range(5):
            FX[5 + q, at, :] = fy[q]
        for q in range(5):
            fzu = lroll(jnp.where(lane == 0, fl[q], fz[q]), 127)
            fyu = FX[5 + q, pl.ds(x * 8 + 1, 8), :]
            HR[q, at, :] = (fz[q] - fzu) + (fy[q] - fyu)

    for x in columns:
        body(x)
    if last:
        low, high = pl.ds(0, 32), pl.ds(8, 32)
        for q in range(5):
            HR[q, low, :] = HR[q, low, :] + (FX[q, low, :] - FX[q, high, :])


def field_stage(EC, EH, EZ, HR):
    lane = lanes()

    def ec(i, x, dy=0):
        return EC[i, pl.ds(8 + (x + 2) * 8 + dy, 8), :]

    def eh(i, x, dy=0):
        return EH[i, pl.ds(8 + (x + 1) * 8 + dy, 8), :]

    for x in range(5):
        at = pl.ds(x * 8, 8)
        EZ[0, at, :] = 0.25 * (ec(2, x - 1, -1) + ec(2, x, -1) + ec(2, x - 1) + ec(2, x))
        s = ec(1, x - 1) + ec(1, x)
        h = eh(1, x - 1) + eh(1, x)
        EZ[1, at, :] = 0.25 * (shifted(s, h, -1, lane) + s)
        EZ[2, at, :] = 0.25 * (shifted(s, h, 1, lane) + s)
        if x < 4:
            s = ec(0, x, -1) + ec(0, x)
            h = eh(0, x, -1) + eh(0, x)
            EZ[3, at, :] = 0.25 * (shifted(s, h, -1, lane) + s)
            EZ[4, at, :] = 0.25 * (shifted(s, h, 1, lane) + s)
    for x in range(4):
        at, up, yu = pl.ds(x * 8, 8), pl.ds(x * 8 + 8, 8), pl.ds(x * 8 + 1, 8)
        ez = EZ[0, at, :]
        HR[5, at, :] = (EZ[2, at, :] - EZ[1, at, :]) - (EZ[0, yu, :] - ez)
        HR[6, at, :] = (EZ[0, up, :] - ez) - (EZ[4, at, :] - EZ[3, at, :])
        HR[7, at, :] = (EZ[3, yu, :] - EZ[3, at, :]) - (EZ[1, up, :] - EZ[1, at, :])


def sym(values):
    return [[values[slot(i, j)] for j in range(3)] for i in range(3)]


def trace(inv, m):
    return (
        inv[0][0] * m[0][0]
        + inv[1][1] * m[1][1]
        + inv[2][2] * m[2][2]
        + 2.0 * (inv[0][1] * m[0][1] + inv[0][2] * m[0][2] + inv[1][2] * m[1][2])
    )


def inverse(g):
    c00 = g[1][1] * g[2][2] - g[1][2] * g[1][2]
    c01 = g[0][2] * g[1][2] - g[0][1] * g[2][2]
    c02 = g[0][1] * g[1][2] - g[0][2] * g[1][1]
    c11 = g[0][0] * g[2][2] - g[0][2] * g[0][2]
    c12 = g[0][1] * g[0][2] - g[0][0] * g[1][2]
    c22 = g[0][0] * g[1][1] - g[0][1] * g[0][1]
    r = 1.0 / (g[0][0] * c00 + g[0][1] * c01 + g[0][2] * c02)
    return sym([c00 * r, c01 * r, c02 * r, c11 * r, c12 * r, c22 * r])


R3 = range(3)


def algebra_stage(G, PR, HR, o_st, o_fl, RT):
    low = rows_iota() < 4

    def body(h, carry):
        x = 2 * h

        def fold(a, b):
            return jnp.where(low, a, b)

        at = aligned(8 * h)

        def strip(ref, q, pad):
            return fold(
                ref[q, pl.ds(pad + x * 8 + 2, 8), :], ref[q, pl.ds(pad + x * 8 + 8 - 2, 8), :]
            )

        def g(q, v):
            t, s = PLACE[v]
            return G[pl.ds(((q * 3 + t - 1) * 16 + 8 * h) * 8 + s, 8, stride=8), :]

        cur = [o_st[v, at, :] for v in range(22)]
        flu = [o_fl[v, at, :] for v in range(8)]
        prims = [strip(PR, q, 8 + 16) for q in range(8)]

        def grad(v):
            return [g(k, v) for k in R3]

        def hess(v):
            return sym([g(4 + s, v) for s in range(6)])

        chi, lapse = cur[0], cur[7]
        metric = sym(cur[1:7])
        shift = cur[8:11]
        khat, theta = cur[11], cur[21]
        trl = sym(cur[12:18])
        conn = cur[18:21]
        inv = inverse(metric)
        ichi = 1.0 / chi
        root = chi * jnp.sqrt(chi)
        ktot = khat + 2.0 * theta

        lor, lor_sq, vel, b0, b, bsq, enth, inertia, ptot = stress_parts(
            prims[0], prims[1], prims[2:5], prims[5:8]
        )
        wl = inertia * lor_sq
        stress = sym(
            [
                wl * vel[i] * vel[j] - b[i] * b[j] + (ptot if i == j else 0.0)
                for i, j in PAIRS
            ]
        )
        total = flu[4] + flu[0]
        dens = total * root
        mom = [flu[1 + i] * root for i in R3]
        dal = grad(7)
        dsh = [grad(8 + i) for i in R3]
        hydro = [strip(HR, q, 0) for q in range(8)]
        for i in R3:
            hydro[1 + i] = (
                hydro[1 + i]
                - total * dal[i]
                + (flu[1] * dsh[0][i] + flu[2] * dsh[1][i] + flu[3] * dsh[2][i])
            )
        third = ktot * (1.0 / 3.0)
        curv = sym([(trl[i][j] + metric[i][j] * third) * ichi for i, j in PAIRS])
        tk = (
            stress[0][0] * curv[0][0]
            + stress[1][1] * curv[1][1]
            + stress[2][2] * curv[2][2]
            + 2.0
            * (stress[0][1] * curv[0][1] + stress[0][2] * curv[0][2] + stress[1][2] * curv[1][2])
        )
        hydro[4] = hydro[4] + lapse / root * tk - dot3(flu[1:4], dal)
        for q in range(8):
            RT[22 + q, at, :] = hydro[q]

        def adv(gr):
            return shift[0] * gr[0] + shift[1] * gr[1] + shift[2] * gr[2]

        def emit(v, rate):
            RT[v, at, :] = rate + g(3, v)

        dg = [[grad(1 + slot(i, j)) if i <= j else None for j in R3] for i in R3]
        dg = [[dg[min(i, j)][max(i, j)] for j in R3] for i in R3]
        lowered = [
            sym([0.5 * (dg[i][k][j] + dg[i][j][k] - dg[j][k][i]) for j, k in PAIRS]) for i in R3
        ]
        raised = [
            sym(
                [
                    inv[i][0] * lowered[0][j][k]
                    + inv[i][1] * lowered[1][j][k]
                    + inv[i][2] * lowered[2][j][k]
                    for j, k in PAIRS
                ]
            )
            for i in R3
        ]
        gd = [trace(inv, raised[i]) for i in R3]
        dchi = grad(0)
        hchi = hess(0)
        xcov = sym(
            [hchi[i][j] - dot3([raised[k][i][j] for k in R3], dchi) for i, j in PAIRS]
        )
        chi_lap = trace(inv, xcov)
        uchi = [dot3(inv[i], dchi) for i in R3]
        chi_sq = dot3(uchi, dchi)
        cross = dot3(uchi, dal)
        hal = hess(7)
        half_ichi = 0.5 * ichi
        lcov = sym(
            [
                hal[i][j]
                - dot3([raised[k][i][j] for k in R3], dal)
                + (dchi[i] * dal[j] + dchi[j] * dal[i] - metric[i][j] * cross) * half_ichi
                for i, j in PAIRS
            ]
        )
        lapse_lap = chi * trace(inv, lcov)
        dgam = [grad(18 + i) for i in R3]
        cu = [
            [
                [
                    inv[l][0] * lowered[j][k][0]
                    + inv[l][1] * lowered[j][k][1]
                    + inv[l][2] * lowered[j][k][2]
                    for l in R3
                ]
                for k in R3
            ]
            for j in R3
        ]
        quarter = half_ichi * half_ichi
        ricci = []
        for i, j in PAIRS:
            v = 1 + slot(i, j)
            hg = hess(v)
            r = -0.5 * trace(inv, hg)
            for k in R3:
                r = r + 0.5 * (metric[k][i] * dgam[k][j] + metric[k][j] * dgam[k][i])
                r = r + 0.5 * gd[k] * (lowered[i][j][k] + lowered[j][i][k])
            for k in R3:
                for l in R3:
                    r = r + raised[k][l][i] * cu[j][k][l]
                    r = r + raised[k][l][j] * cu[i][k][l]
                    r = r + raised[k][i][l] * cu[k][j][l]
            r = r + (xcov[i][j] + metric[i][j] * chi_lap) * half_ichi
            r = r - (dchi[i] * dchi[j] + 3.0 * metric[i][j] * chi_sq) * quarter
            ricci.append(r)
        ricci = sym(ricci)
        rscal = chi * trace(inv, ricci)
        strace = chi * trace(inv, stress)
        mixed = [[dot3(inv[i], [trl[k][j] for k in R3]) for j in R3] for i in R3]
        up = sym([dot3(mixed[i], inv[j]) for i, j in PAIRS])
        aa = trace(trl, up)
        div = dsh[0][0] + dsh[1][1] + dsh[2][2]
        div23 = (2.0 / 3.0) * div

        emit(0, adv(dchi) + (2.0 / 3.0) * chi * (lapse * ktot - div))
        emit(7, adv(dal) - 2.0 * lapse * khat)
        for i in R3:
            emit(8 + i, adv(dsh[i]) + 0.75 * conn[i] - shift[i])
        dkh = grad(11)
        dth = grad(21)
        emit(
            11,
            adv(dkh)
            - lapse_lap
            + lapse * (aa + ktot * third)
            + FOUR_PI * lapse * (strace + dens)
            + 0.02 * lapse * theta,
        )
        src = sym(
            [
                -lcov[i][j] + lapse * (ricci[i][j] - (2.0 * FOUR_PI) * stress[i][j])
                for i, j in PAIRS
            ]
        )
        strc = trace(inv, src) * (1.0 / 3.0)
        for i, j in PAIRS:
            s = slot(i, j)
            acc = adv(dg[i][j])
            for k in R3:
                acc = acc + metric[i][k] * dsh[k][j] + metric[j][k] * dsh[k][i]
            emit(1 + s, acc - metric[i][j] * div23 - 2.0 * lapse * trl[i][j])
            prod = dot3(trl[i], [mixed[k][j] for k in R3])
            acc = adv(grad(12 + s))
            for k in R3:
                acc = acc + trl[i][k] * dsh[k][j] + trl[j][k] * dsh[k][i]
            emit(
                12 + s,
                acc
                - trl[i][j] * div23
                + chi * (src[i][j] - metric[i][j] * strc)
                + lapse * (ktot * trl[i][j] - 2.0 * prod),
            )
        hsh = [hess(8 + i) for i in R3]
        ddiv = [hsh[0][0][j] + hsh[1][1][j] + hsh[2][2][j] for j in R3]
        for i in R3:
            br = trace(up, raised[i])
            br = br - 1.5 * ichi * dot3(up[i], dchi)
            br = br - (1.0 / 3.0) * dot3(inv[i], [2.0 * dkh[j] + dth[j] for j in R3])
            br = br - (2.0 * FOUR_PI) * dot3(inv[i], mom)
            emit(
                18 + i,
                adv(dgam[i])
                - dot3(gd, dsh[i])
                + gd[i] * div23
                + trace(inv, hsh[i])
                + (1.0 / 3.0) * dot3(inv[i], ddiv)
                - 2.0 * dot3(up[i], dal)
                + 2.0 * lapse * br
                - 0.04 * lapse * (conn[i] - gd[i]),
            )
        emit(
            21,
            adv(dth)
            + 0.5
            * lapse
            * (rscal - aa + (2.0 / 3.0) * ktot * ktot - (4.0 * FOUR_PI) * dens)
            - 0.04 * lapse * theta,
        )
        return carry

    lax.fori_loop(0, 2, body, 0)


def compute_scratch():
    V = lambda *s: pltpu.VMEM(s, jnp.float32)
    return [
        V(10 * 3 * 16 * 8, 128),
        V(8, 80, 128),
        V(8, 64, 128),
        V(3, 80, 128),
        V(3, 64, 128),
        V(10, 48, 128),
        V(8, 48, 128),
        V(5, 48, 128),
    ]


MESH = pl.DeviceIdType.MESH
PHASES = ((0, 1), (1, 7), (8, 7), (15, 7))
N_SLOTS = 22
N_GREETED = 18


def wave_stage(own):
    metric = sym([own(8 + v) for v in range(1, 7)])
    inv = inverse(metric)
    scale = 2.0 * own(8 + 7) * own(8)
    speeds = [jnp.abs(own(16 + d)) + jnp.sqrt(scale * inv[d][d]) for d in range(3)]
    return jnp.maximum(jnp.maximum(speeds[0], speeds[1]), speeds[2])


def load_stage(st, fl, o_st, o_fl, T, tiles):
    for u in range(30):
        src, dst, v = (fl, o_fl, u) if u < 8 else (st, o_st, u - 8)
        t, s = (0, u) if u < 8 else PLACE[v]
        if t not in tiles:
            continue
        for x in range(4):
            value = src[v, x]
            T[pl.ds(row_of(t, x + 3, 4) + s, 4, stride=8), :] = value
            dst[v, pl.ds(4 * x, 4), :] = value


def speed_stage(st, mine):
    top = None
    for x in range(4):

        def own(u):
            return st[u - 8, x]

        speed = wave_stage(own)
        top = speed if top is None else jnp.maximum(top, speed)
    mine[0] = jnp.max(top, axis=0, keepdims=True)


def border_stage(o_st, o_fl, zsend):
    lane = lanes()

    def body(h, carry):
        at = pl.ds(pl.multiple_of(8 * h, 8), 8)
        last = jnp.zeros((8, 128), jnp.float32)
        first = jnp.zeros((8, 128), jnp.float32)
        for u in range(30):
            t, s = (0, u) if u < 8 else PLACE[u - 8]
            p = PACK - 3 * (8 * t + s)
            here = (lane >= p) & (lane < p + 3)
            value = o_fl[u, at, :] if u < 8 else o_st[u - 8, at, :]
            first = jnp.where(here, lroll(value, p), first)
            last = jnp.where(here, lroll(value, p - 125), last)
        zsend[0, at, :] = last
        zsend[1, at, :] = first
        return carry

    lax.fori_loop(0, 2, body, 0)


def halo_rows(zrecv, T):
    for side in range(2):
        for x in range(4):
            T[pl.ds(row_of(Z_TILE, x + 3, 4) + 6 + side, 4, stride=8), :] = zrecv[
                side, pl.ds(4 * x, 4), :
            ]


def kernel(st_in, fl_in, o_st, o_fl, st, fl, insem, T5, zsend, zrecv, mine, slots, RT, ssem, rsem, msem, known, *scratch):
    gx, gy, gz = lax.axis_index("gx"), lax.axis_index("gy"), lax.axis_index("gz")
    hi, core = gy & 1, gx & 1
    T = T5.reshape(3840, 128)

    def at_x(step):
        x2 = (hi * 4 + gz + step) & 7
        return (gx, gy - hi + (x2 >> 2), x2 & 3)

    mate = (gx + 1 - 2 * core, gy, gz)
    ring_x = [at_x(k) for k in range(1, 8)]
    ring_y = [(gx, (gy + 2 * k) & 15, gz) for k in range(1, 8)]
    ring_z = [((gx + 2 * k) & 15, gy, gz) for k in range(1, 8)]
    x_up, x_dn = ((gx + 1) & 15, gy, gz), ((gx + 15) & 15, gy, gz)
    z_up, z_dn = (gx, gy, (gz + 1) & 3), (gx, gy, (gz + 3) & 3)
    y_up, y_dn = ring_y[0], ring_y[6]
    cross = ((gx + 15 + 2 * core) & 15, gy, gz)
    partner = ring_x[3]
    onward = (gx, (gy + 2 - 4 * hi) & 15, gz)

    barrier = pltpu.get_barrier_semaphore()
    for peer in [partner, mate, cross, y_up, y_dn] + ring_x[:3] + ring_x[4:] + ring_z:
        pl.semaphore_signal(barrier, inc=1, device_id=peer, device_id_type=MESH)
    fetched = [
        pltpu.make_async_copy(st_in, st, insem.at[0]),
        pltpu.make_async_copy(fl_in, fl, insem.at[1]),
    ]
    for copy in fetched:
        copy.start()
    fetched[0].wait()
    speed_stage(st, mine)
    load_stage(st, fl, o_st, o_fl, T, (1,))
    fetched[1].wait()
    load_stage(st, fl, o_st, o_fl, T, (0,))
    load_stage(st, fl, o_st, o_fl, T, (2, 3))
    border_stage(o_st, o_fl, zsend)
    pl.semaphore_wait(barrier, N_GREETED)

    def tell(step):
        for peer in (y_up, y_dn):
            pl.semaphore_signal(known.at[step], inc=1, device_id=peer, device_id_type=MESH)

    def told(step):
        pl.semaphore_wait(known.at[step], 2)

    started = []

    def send(src, dst, peer):
        k = len(started)
        copy = pltpu.make_async_remote_copy(
            src_ref=src,
            dst_ref=dst,
            send_sem=ssem.at[k],
            recv_sem=rsem.at[k],
            device_id=peer,
            device_id_type=MESH,
        )
        copy.start()
        started.append(copy)
        return copy

    def share(phase, peers):
        base = PHASES[phase][0]
        for k, peer in enumerate(peers):
            pltpu.make_async_remote_copy(
                src_ref=mine.at[phase],
                dst_ref=slots.at[base + k],
                send_sem=msem.at[phase],
                recv_sem=msem.at[4 + phase],
                device_id=peer,
                device_id_type=MESH,
            ).start()

    def gathered(phase):
        part = slots.at[pl.ds(*PHASES[phase])]
        pltpu.make_async_copy(part, part, msem.at[4 + phase]).wait()
        mine[phase + 1] = jnp.maximum(mine[phase], jnp.max(slots[pl.ds(*PHASES[phase])], axis=0))

    def drained(phase):
        part = slots.at[pl.ds(*PHASES[phase])]
        pltpu.make_async_copy(part, part, msem.at[phase]).wait()

    def block(t, n, xp, nx, yp, ny):
        return T5.at[pl.ds(t, n), pl.ds(xp, nx), pl.ds(yp, ny)]

    def to_partner(t):
        return send(block(t, 1, 3, 4, 4, 4), block(t, 1, 3, 4, 8 * hi, 4), partner)

    def go_on(t):
        return send(block(t, 1, 3, 4, 9 - 9 * hi, 3), block(t, 1, 3, 4, 1 + 7 * hi, 3), onward)

    def faces(t, n):
        return [
            send(block(t, n, 3, 3, 4, 4), block(t, n, 7, 3, 4, 4), x_dn),
            send(block(t, n, 4, 3, 4, 4), block(t, n, 0, 3, 4, 4), x_up),
        ]

    def edges(t, n):
        copies = []
        for yp in (2, 8):
            copies.append(send(block(t, n, 3, 2, yp, 2), block(t, n, 7, 2, yp, 2), x_dn))
            copies.append(send(block(t, n, 5, 2, yp, 2), block(t, n, 1, 2, yp, 2), x_up))
        return copies

    G, PR, PH, EC, EH, FX, HR, EZ = scratch
    far, relay, side = {}, {}, {}
    share(0, [mate])
    tell(0)
    zs = [send(zsend.at[0], zrecv.at[0], z_up), send(zsend.at[1], zrecv.at[1], z_dn)]
    for t in range(2):
        far[t] = to_partner(t)
    front = faces(0, 2)
    for copy in zs:
        copy.wait_recv()
    halo_rows(zrecv, T)
    for t in (2, 3):
        far[t] = to_partner(t)
    gathered(0)
    share(1, ring_z)
    front += faces(2, 2)
    told(0)
    tell(1)
    far[0].wait_recv()
    relay[0] = go_on(0)
    gathered(1)
    share(2, ring_x)
    told(1)
    tell(2)
    far[1].wait_recv()
    relay[1] = go_on(1)
    far[2].wait_recv()
    relay[2] = go_on(2)
    for copy in front:
        copy.wait_recv()
    deriv_xz(T, G, (1, 2, 3))
    for t in range(2):
        relay[t].wait_recv()
        side[t] = edges(t, 1)
    gathered(2)
    told(2)
    share(3, ring_y)
    far[3].wait_recv()
    relay[3] = go_on(3)
    relay[2].wait_recv()
    side[2] = edges(2, 1)
    prim_stage(T, PR, PH, EC, EH, (2, 3, 4), (1, 2, 3))
    flux_stage(T, PR, PH, FX, HR, (0, 1, 2), False)
    relay[3].wait_recv()
    deriv_y(T, G, (1, 2, 3))
    for t in range(3):
        for copy in side[t]:
            copy.wait_recv()
    deriv_xy(T, G, (1, 2))
    prim_stage(T, PR, PH, EC, EH, (0, 1, 5, 6, 7), (0, 4, 5))
    flux_stage(T, PR, PH, FX, HR, (3,), True)
    field_stage(EC, EH, EZ, HR)
    algebra_stage(G, PR, HR, o_st, o_fl, RT)
    gathered(3)
    step = 0.25 / jnp.max(mine[4], axis=1, keepdims=True)
    for v in range(22):
        o_st[v] = o_st[v] + step * RT[v]
    for v in range(8):
        o_fl[v] = o_fl[v] + step * RT[22 + v]
    for copy in started:
        copy.wait_send()
    for phase in range(4):
        drained(phase)


def per_device(spacetime, fluid):
    vmem = pl.BlockSpec(memory_space=pltpu.VMEM)
    space = lambda *s: pltpu.VMEM(s, jnp.float32)
    st_new, fl_new = pl.pallas_call(
        kernel,
        out_shape=(
            jax.ShapeDtypeStruct((22, 16, 128), jnp.float32),
            jax.ShapeDtypeStruct((8, 16, 128), jnp.float32),
        ),
        in_specs=[pl.BlockSpec(memory_space=pltpu.HBM)] * 2,
        out_specs=(vmem, vmem),
        scratch_shapes=[
            space(22, 4, 4, 128),
            space(8, 4, 4, 128),
            pltpu.SemaphoreType.DMA((2,)),
            space(4, PADX, PADY, 8, 128),
            space(2, 16, 128),
            space(2, 16, 128),
            space(5, 1, 128),
            space(N_SLOTS, 1, 128),
            space(30, 16, 128),
            pltpu.SemaphoreType.DMA((32,)),
            pltpu.SemaphoreType.DMA((32,)),
            pltpu.SemaphoreType.DMA((8,)),
            pltpu.SemaphoreType.REGULAR((3,)),
        ]
        + compute_scratch(),
        compiler_params=pltpu.CompilerParams(
            collective_id=1, has_side_effects=True, vmem_limit_bytes=56164352
        ),
    )(spacetime, fluid)
    return st_new.reshape(22, 4, 4, 128), fl_new.reshape(8, 4, 4, 128)


def solution(mesh):
    spec = P(None, "gx", "gy", "gz")
    return jax.shard_map(
        per_device, mesh=mesh, in_specs=(spec, spec), out_specs=(spec, spec), check_vma=False
    )
```
